32 devices in a mesh: member: 2 (over x), lat: 8 (over z, y), lon: 2 (over core).
Axes of the slice: x: 2, y: 2, z: 4, core: 2. Of those that a mesh axis runs over, the one named last changes fastest.
Arguments:
- tokens: bfloat16 [128, 192, 1024], P(('member', 'lat'), 'lon'), parts along dimension 0, may hold values from -6 to 6
- ln_gain: float32 [1024], replicated, may hold values from 0.5 to 1.5
- w_query: bfloat16 [1024, 1024], replicated, may hold values from -3 to 3
- w_keyval: bfloat16 [1024, 2048], replicated, may hold values from -3 to 3
- w_out: bfloat16 [1024, 1024], replicated, may hold values from -0.1875 to 0.1875
- w_dec: bfloat16 [1024, 512], replicated, may hold values from -0.1875 to 0.1875
- nudge: float32 [32], replicated, may hold values from 0.2 to 1
- state: float32 [32, 512, 768], P(None, ('member', 'lat'), 'lon'), parts along dimension 1, may hold values from -6 to 6
Outputs:
- advanced: float32 [32, 512, 768], P(None, ('member', 'lat', 'lon')), parts along dimension 1
The draws below stay inside these ranges and needn't reach their ends.
There are 2 independent parts, one for each index of `member`. The reference program is written for one: setup_inputs(seed, part) draws one part's arguments, and reference() takes and returns one part's arrays. A program takes and returns all parts, laid end to end along the dimension named above; an argument that names none is the same for every part. Nothing has to cross between parts.
All inputs are finite; a program needn't handle non-finite values.
Results may differ from the reference program's by a relative error of at most 0.003.
Values may be sent and summed in bfloat16 or wider, within the bound.
A program may use at most 128 MiB of HBM per device.

```python
import math
import jax
import jax.numpy as jnp
from jax import lax

D = 1024
HEADS = 16
WIN = 8
PATCH = 4
VARS = 4
LEV = 8
LON_PIX = 768
KEEP = 256
CH = 32
NTR = 64
NTC = 192
NLAT_PIX = 256


def paired_weights(key):
    base_key = jax.random.fold_in(key, 1234)
    key_keys, key_query = jax.random.split(base_key, 2)
    keyval_raw = jax.random.normal(key_keys, (D, 2 * D), jnp.float32) / math.sqrt(D)
    query_raw = jax.random.normal(key_query, (D, D), jnp.float32) / math.sqrt(D)
    return (jnp.clip(query_raw, -3.0, 3.0), jnp.clip(keyval_raw, -3.0, 3.0))


def draw_w_query(key, part):
    return paired_weights(key)[0].astype(jnp.bfloat16)


def draw_w_keyval(key, part):
    return paired_weights(key)[1].astype(jnp.bfloat16)


def block_scale(key, dims, pieces, least, largest):
    def one(axis_at, parts):
        heights = jax.random.uniform(jax.random.fold_in(jax.random.fold_in(key, 6), axis_at), (parts,), jnp.float32, least / len(pieces), largest / len(pieces))
        return jnp.repeat(jnp.exp(heights), dims[axis_at] // parts).reshape((-1,) + (1,) * (len(dims) - axis_at - 1))

    gain = one(*pieces[0])
    for cut in pieces[1:]:
        gain = gain * one(*cut)
    return gain


def normal_values(own_key, shape, deviation, limit, cuts=(), held_as=jnp.bfloat16):
    result = jax.random.normal(own_key, shape, jnp.float32) * deviation
    if len(cuts) > 0:
        result = block_scale(own_key, shape, cuts, -0.22, 0.18) * result
    return jnp.clip(result, min=-limit, max=limit).astype(held_as)


def setup_inputs(seed: int = 0, part: int = 0) -> dict:
    splits = jax.random.split(jax.random.key(seed), 9)
    part_keys = jax.random.split(jax.random.fold_in(splits[8], part), 9)
    return {
        "tokens": normal_values(part_keys[0], (NTR, NTC, D), 1.0, 6.0, ((0, 8), (1, 2))),
        "ln_gain": jnp.clip(1.0 + 0.1 * jax.random.normal(splits[1], (D,), jnp.float32), 0.5, 1.5),
        "w_query": draw_w_query(jax.random.fold_in(splits[8], 71), part),
        "w_keyval": draw_w_keyval(jax.random.fold_in(splits[8], 71), part),
        "w_out": normal_values(splits[4], (D, D), D ** -0.5, 0.1875),
        "w_dec": normal_values(splits[5], (D, CH * PATCH * PATCH), D ** -0.5, 0.1875),
        "nudge": jnp.clip(jnp.exp(jax.random.uniform(splits[6], (CH,), jnp.float32, math.log(0.2), math.log(1.0))), 0.2, 1.0),
        "state": normal_values(part_keys[7], (CH, NLAT_PIX, LON_PIX), 1.0, 6.0, ((1, 8), (2, 2)), jnp.float32),
    }


time_step = 0.1
diffusion = 0.5
epsilon = 1e-05

def layer_norm(inputs, gain_vector):
    centred = inputs - lax.optimization_barrier(jnp.mean(inputs, axis=-1, keepdims=True))
    variance = lax.optimization_barrier(jnp.mean(centred * centred, axis=-1, keepdims=True))
    return (centred * lax.rsqrt(variance + epsilon) * gain_vector).astype(jnp.bfloat16)

def to_windows(tensor, row_blocks, col_blocks):
    features = tensor.shape[-1]
    shaped = tensor.reshape(row_blocks, WIN, col_blocks, WIN, features)
    return shaped.transpose(0, 2, 1, 3, 4).reshape(row_blocks * col_blocks, WIN * WIN, features)

def from_windows(tensor, row_blocks, col_blocks):
    features = tensor.shape[-1]
    shaped = tensor.reshape(row_blocks, col_blocks, WIN, WIN, features)
    return shaped.transpose(0, 2, 1, 3, 4).reshape(row_blocks * WIN, col_blocks * WIN, features)

def window_attention(queries, keys_win, values_win, key_valid):
    windows_count, window_cells, model_width = queries.shape
    head_size = model_width // HEADS
    query_heads = queries.astype(jnp.float32).reshape(windows_count, window_cells, HEADS, head_size)
    key_heads = keys_win.astype(jnp.float32).reshape(windows_count, window_cells, HEADS, head_size)
    value_heads = values_win.astype(jnp.float32).reshape(windows_count, window_cells, HEADS, head_size)
    scores = jnp.einsum('wqhd,wkhd->whqk', query_heads, key_heads) / math.sqrt(head_size)
    scores = jnp.where(key_valid[:, None, None, :], scores, -1e+30)
    peak_score = lax.optimization_barrier(jnp.max(scores, axis=-1, keepdims=True))
    weights = jnp.exp(scores - peak_score)
    weights = (weights / lax.optimization_barrier(jnp.sum(weights, axis=-1, keepdims=True))).astype(jnp.bfloat16)
    weights = lax.optimization_barrier(weights).astype(jnp.float32)
    mixed_out = jnp.einsum('whqk,wkhd->wqhd', weights, value_heads)
    return mixed_out.astype(jnp.bfloat16).reshape(windows_count, window_cells, model_width)

def zonal_basis(length, kept_waves):
    columns = jnp.arange(length, dtype=jnp.int32)
    wave_index = jnp.arange(kept_waves, dtype=jnp.int32)
    winding = columns[:, None] * wave_index[None, :] % length
    phases = winding.astype(jnp.float32) * (2.0 * math.pi / length)
    basis_table = jnp.concatenate([jnp.cos(phases), jnp.sin(phases)], axis=1)
    factor = jnp.where(wave_index == 0, 1.0, 2.0).astype(jnp.float32) / length
    return (basis_table, jnp.concatenate([factor, factor]))

def tendency(padded):
    centre = padded[:, 1:-1, 1:-1]
    east_cell = padded[:, 1:-1, 2:]
    west_cell = padded[:, 1:-1, :-2]
    north_cell = padded[:, 2:, 1:-1]
    south_cell = padded[:, :-2, 1:-1]
    field_shape = (VARS, LEV) + centre.shape[1:]
    wind_u = centre[:LEV][None]
    wind_v = centre[LEV:2 * LEV][None]
    advection = wind_u * (east_cell - west_cell).reshape(field_shape) * 0.5
    advection = advection + wind_v * (north_cell - south_cell).reshape(field_shape) * 0.5
    spread_term = diffusion * (east_cell + west_cell + north_cell + south_cell - 4.0 * centre)
    return spread_term - advection.reshape(centre.shape)

def extend_full(field):
    padded_rows = jnp.pad(field, ((0, 0), (1, 1), (0, 0)))
    return jnp.concatenate([padded_rows[..., -1:], padded_rows, padded_rows[..., :1]], axis=2)

def reference(tokens, ln_gain, w_query, w_keyval, w_out, w_dec, nudge, state):
    rows_all, cols_all, model_width = tokens.shape
    half_win = WIN // 2
    padded = jnp.pad(tokens, ((half_win, half_win), (0, 0), (0, 0)))
    padded = jnp.roll(padded, half_win, axis=1)
    inside = jnp.pad(jnp.ones((rows_all,), jnp.int32), (half_win, half_win))
    col_blocks = cols_all // WIN

    def one_band(band_index):
        row_start = (band_index * WIN).astype(jnp.int32)
        token_band = lax.dynamic_slice_in_dim(padded, row_start, WIN, 0)
        row_keep = lax.dynamic_slice_in_dim(inside, row_start, WIN, 0)
        normed = layer_norm(token_band.astype(jnp.float32), ln_gain)
        flat_rows = normed.reshape(WIN * cols_all, model_width)
        queries = jnp.dot(flat_rows, w_query, preferred_element_type=jnp.float32).astype(jnp.bfloat16)
        keyval = jnp.dot(flat_rows, w_keyval, preferred_element_type=jnp.float32).astype(jnp.bfloat16)
        queries = queries.reshape(WIN, cols_all, model_width)
        keyval = keyval.reshape(WIN, cols_all, 2 * model_width)
        keep_grid = jnp.broadcast_to(row_keep[:, None, None], (WIN, cols_all, 1))
        key_valid = to_windows(keep_grid, 1, col_blocks)[..., 0] > 0
        keyval_win = to_windows(keyval, 1, col_blocks)
        outputs = window_attention(to_windows(queries, 1, col_blocks), keyval_win[..., :model_width], keyval_win[..., model_width:], key_valid)
        return from_windows(outputs, 1, col_blocks)
    all_bands = lax.map(one_band, jnp.arange(rows_all // WIN + 1, dtype=jnp.int32))
    attended = all_bands.reshape(rows_all + WIN, cols_all, model_width)[half_win:half_win + rows_all]
    attended = jnp.roll(attended, -half_win, axis=1)
    update = jnp.dot(attended.reshape(-1, model_width), w_out, preferred_element_type=jnp.float32)
    layer_out = (tokens.astype(jnp.float32).reshape(-1, model_width) + update).astype(jnp.bfloat16)
    decoded = jnp.dot(layer_out, w_dec, preferred_element_type=jnp.float32)
    decoded = decoded.reshape(rows_all, cols_all, VARS * LEV, PATCH, PATCH).transpose(2, 0, 3, 1, 4)
    decoded = decoded.reshape(VARS * LEV, rows_all * PATCH, cols_all * PATCH)
    basis_table, factor = zonal_basis(LON_PIX, KEEP)
    difference = (decoded - state).reshape(-1, LON_PIX)
    coefficients = jnp.dot(difference, basis_table, precision=lax.Precision.HIGHEST, preferred_element_type=jnp.float32)
    filtered = jnp.dot(coefficients * factor, basis_table.T, precision=lax.Precision.HIGHEST, preferred_element_type=jnp.float32)
    nudged = state + nudge[:, None, None] * filtered.reshape(state.shape)
    first_section = nudged + time_step * tendency(extend_full(nudged))
    return 0.5 * (nudged + first_section + time_step * tendency(extend_full(first_section)))
```

```python
import functools
import math

import jax
import jax.numpy as jnp
import ml_dtypes
import numpy as np
from jax import lax
from jax.experimental import pallas as pl
from jax.experimental.pallas import tpu as pltpu
from jax.sharding import PartitionSpec as P

HEADS = 16
WIN = 8
PATCH = 4
VARS = 4
LEV = 8
KEEP = 256

time_step = 0.1
diffusion = 0.5
epsilon = 1e-05
F32 = jnp.float32
BF16 = jnp.bfloat16
NT = (((1,), (1,)), ((), ()))
HALF = WIN // 2
MESH = pl.DeviceIdType.MESH


def chunk_bounds(windows):
    size = 4
    return [(w, min(w + size, windows)) for w in range(0, windows, size)]


def filter_tables(length, kept, windows):
    offset = np.arange(length)
    waves = np.arange(1, kept)
    angles = 2.0 * np.pi * ((offset[:, None] * waves[None, :]) % length) / length
    kernel = (1.0 + 2.0 * np.cos(angles).sum(1)) / length
    pixel = []
    for side in range(2):
        for w0, w1 in chunk_bounds(windows):
            for b in range(PATCH):
                column = np.arange(w0 * WIN, w1 * WIN) + HALF
                pixel.append(side * (length // 2) + PATCH * column + b)
    pixel = np.concatenate(pixel)
    plain = (offset[None, :] - offset[:, None]) % length
    patch = (offset[None, :] - pixel[:, None]) % length

    def rounded(factor):
        return (kernel * factor).astype(np.float32).astype(ml_dtypes.bfloat16)

    factors = 1.0 + np.arange(2048) / 2048
    errors = [np.square(rounded(f).astype(np.float64) / f - kernel).sum() for f in factors]
    factor = float(factors[int(np.argmin(errors))])
    return rounded(factor)[plain], rounded(factor)[patch], 1.0 / factor


def tendency_row(south, centre, north):
    channels, length = centre.shape
    west = pltpu.roll(centre, 1, 1)
    east = pltpu.roll(centre, length - 1, 1)
    u = centre[:LEV][None]
    v = centre[LEV : 2 * LEV][None]
    dx = (east - west).reshape(VARS, LEV, length)
    dy = (north - south).reshape(VARS, LEV, length)
    advection = ((u * dx + v * dy) * 0.5).reshape(channels, length)
    return diffusion * (east + west + north + south - 4.0 * centre) - advection


def cycle_kernel(
    n_lat, undo, tokens, state, wq_hbm, wkv_hbm, wo_hbm, wd_hbm, plain_hbm, patch_hbm, gain_ref, nudge_ref, out_ref,
    wqkv, wo, wd, wdt, plain, patch, own, halo, side, strip_own, strip_far, edge_own, edge_halo,
    xs, normed, qkv, att, lo, bias, band, base, sent, came, held, up_rows, down_rows, before, after, first, strength,
    load_sem, send_sem, recv_sem,
):
    lat, lon = lax.axis_index("lat"), lax.axis_index("lon")
    peer = 1 - lon
    cols, width = tokens.shape[1:]
    windows = cols // WIN
    cells = 2 * HALF * WIN
    tall, channels, length = base.shape
    wide = length // 2
    chunks = chunk_bounds(windows)
    count = len(chunks)
    is_low = lon == 0
    has_prev, has_next = lat > 0, lat < n_lat - 1
    prev, nxt = jnp.maximum(lat - 1, 0), jnp.minimum(lat + 1, n_lat - 1)
    inner = jnp.where(is_low, has_prev, has_next)
    more = jnp.where(is_low, has_next, has_prev)
    ring = {"lat": jnp.where(is_low, nxt, prev), "lon": jnp.where(more, lon, peer)}
    mate = {"lat": jnp.where(is_low, prev, nxt), "lon": peer}
    side_by = {"lat": lat, "lon": peer}

    def load(i, src, dst):
        return pltpu.make_async_copy(src, dst, load_sem.at[i])

    def remote(i, src, dst, to):
        return pltpu.make_async_remote_copy(
            src_ref=src, dst_ref=dst, send_sem=send_sem.at[i], recv_sem=recv_sem.at[i],
            device_id=to, device_id_type=MESH,
        )

    own_at = pl.multiple_of(lon * HALF, HALF)
    far_at = pl.multiple_of(peer * HALF, HALF)
    strip = side.shape[1]
    side_load = load(0, tokens.at[pl.ds(far_at, HALF), pl.ds(0, strip), :], side)
    own_load = load(1, tokens.at[pl.ds(own_at, HALF)], own)
    dec_load = load(2, wd_hbm, wd)
    query_load = load(3, wq_hbm, wqkv.at[:, pl.ds(0, width)])
    keyval_load = load(4, wkv_hbm, wqkv.at[:, pl.ds(width, 2 * width)])
    my_rows = pl.ds(pl.multiple_of(lon * tall, 8), tall)
    peer_rows = pl.ds(pl.multiple_of(peer * tall, 8), tall)
    state_load = load(5, state.at[:, my_rows, :], band.at[:, :, pl.ds(0, wide)])
    plain_load = load(6, plain_hbm, plain)
    out_load = load(7, wo_hbm, wo)
    patch_load = load(8, patch_hbm, patch)
    for item in (
        side_load, own_load, dec_load, query_load, keyval_load, state_load, plain_load, out_load, patch_load
    ):
        item.start()

    barrier = pltpu.get_barrier_semaphore()

    def greet(to):
        pl.semaphore_signal(barrier, inc=1, device_id=to, device_id_type=MESH)

    greet(side_by)

    @pl.when(has_prev)
    def _():
        greet({"lat": prev, "lon": lon})

    @pl.when(has_next)
    def _():
        greet({"lat": nxt, "lon": lon})

    @pl.when(inner)
    def _():
        greet(mate)

    pl.semaphore_wait(
        barrier, 1 + has_prev.astype(jnp.int32) + has_next.astype(jnp.int32) + inner.astype(jnp.int32)
    )

    ends = [min(cols, -(-(w1 * WIN + HALF) // strip) * strip) for _, w1 in chunks]
    token_copies = []
    for i, (begin, end) in enumerate(zip([0] + ends[:-1], ends)):
        at = pl.ds(begin, end - begin)
        token_copies.append(remote(i, tokens.at[pl.ds(far_at, HALF), at, :], halo.at[:, at, :], ring))
    for item in token_copies:
        item.start()
    base_id = count
    state_copy = remote(base_id, state.at[:, peer_rows, :], band.at[:, :, pl.ds(wide, wide)], side_by)
    strip_peer = remote(base_id + 1, strip_far, edge_own, side_by)
    strip_mate = remote(base_id + 2, strip_own, edge_halo, mate)
    field_copies = [remote(base_id + 3 + i, sent.at[i], came.at[i], mate) for i in range(count)]
    up_copy_id, down_copy_id = base_id + 3 + count, base_id + 4 + count

    def pack(source, out):
        for r in range(0, HALF, 2):
            pair = [source[r + j, 0:WIN, :].astype(F32)[:HALF] for j in range(2)]
            out[r * HALF : (r + 2) * HALF, :] = jnp.concatenate(pair, axis=0).astype(BF16)

    side_load.wait()
    pack(side, strip_far)
    strip_peer.start()
    own_load.wait()
    pack(own, strip_own)

    @pl.when(inner)
    def _():
        strip_mate.start()

    @pl.when(jnp.logical_not(inner))
    def _():
        edge_halo[...] = strip_own[...]

    state_copy.start()

    def normalize(source, edge, w0, w1, at):
        c0, c1 = w0 * WIN, w1 * WIN
        n = w1 - w0
        for r in range(HALF):
            if c1 < cols:
                block = source[r, c0 : c1 + WIN, :].astype(F32)[HALF : HALF + n * WIN]
            else:
                block = source[r, c0:c1, :].astype(F32)[HALF:]
                r0 = r // 2 * WIN
                tail = edge[r0 : r0 + WIN, :].astype(F32)[r % 2 * HALF : r % 2 * HALF + HALF]
                block = jnp.concatenate([block, tail], axis=0)
            centred = block - jnp.mean(block, axis=-1, keepdims=True)
            variance = jnp.mean(centred * centred, axis=-1, keepdims=True)
            unit = centred * lax.rsqrt(variance + epsilon) * gain_ref[...]
            xs[w0:w1, at + r * WIN : at + (r + 1) * WIN, :] = block.reshape(n, WIN, width)
            normed[w0:w1, r * WIN : (r + 1) * WIN, :] = unit.reshape(n, WIN, width)

    scale = math.log2(math.e) / math.sqrt(width // HEADS)

    def project(w0, w1, at):
        n = w1 - w0
        flat = normed[w0:w1].reshape(n * HALF * WIN, width).astype(BF16)
        for part in range(3):
            on = slice(part * width, (part + 1) * width)
            value = jnp.dot(flat, wqkv[:, on], preferred_element_type=F32)
            if part == 0:
                value = value * scale
            qkv[w0:w1, at : at + HALF * WIN, on] = value.astype(BF16).reshape(n, HALF * WIN, width)

    def attend(w0, w1):
        head = width // HEADS
        pair = 2 * head
        lanes = lax.broadcasted_iota(jnp.int32, (cells, pair), 1) < head
        left = lax.broadcasted_iota(jnp.int32, (2 * cells, pair), 1) < head
        upper = lax.broadcasted_iota(jnp.int32, (2 * cells, pair), 0) < cells
        ones = (left == upper).astype(F32).astype(BF16)

        def both(x):
            zero = jnp.zeros_like(x)
            return jnp.concatenate([jnp.where(lanes, x, zero), jnp.where(lanes, zero, x)], axis=0)

        @pl.loop(w0, w1, unroll=w1 - w0)
        def _(w):
            spots = [p * pair for p in range(HEADS // 2)]
            scores = []
            for on in spots:
                q = qkv[w, :, on : on + pair]
                k = both(qkv[w, :, width + on : width + on + pair])
                scores.append(lax.dot_general(q, k, NT, preferred_element_type=F32) + bias[...])
            powers = []
            for s in scores:
                low = jnp.max(jnp.where(lanes, s, -jnp.inf), axis=-1, keepdims=True)
                high = jnp.max(jnp.where(lanes, -jnp.inf, s), axis=-1, keepdims=True)
                powers.append(jnp.exp2(s - jnp.where(lanes, low, high)).astype(BF16))
            mixed = []
            for on, e in zip(spots, powers):
                v = both(qkv[w, :, 2 * width + on : 2 * width + on + pair])
                o = jnp.dot(e, jnp.concatenate([v, ones], axis=1), preferred_element_type=F32)
                mixed.append((o[:, :pair] / o[:, pair:]).astype(BF16))
            att[w] = jnp.concatenate(mixed, axis=1)

    patches = wdt.shape[0]
    part = PATCH * channels

    def place(value, at, n):
        for r in range(HALF):
            pieces = [value[b * part : (b + 1) * part, r * n : (r + 1) * n] for b in range(PATCH)]
            held[r * part : (r + 1) * part, at : at + PATCH * n] = jnp.concatenate(pieces, axis=1)

    def decode(i):
        w0, w1 = chunks[i]
        n = w1 - w0
        mixed = att[w0:w1].reshape(n * cells, width)
        for at in range(0, width, 512):
            update = jnp.dot(mixed, wo[:, at : at + 512], preferred_element_type=F32)
            value = xs[w0:w1, :, at : at + 512] + update.reshape(n, cells, 512)
            value = value.reshape(n, 2 * HALF, WIN, 512)
            value = jnp.swapaxes(value, 0, 1).reshape(n * cells, 512)
            lo[0 : n * cells, at : at + 512] = value.astype(BF16)
        value = lax.dot_general(wdt[...], lo[0 : n * cells, :], NT, preferred_element_type=F32).astype(BF16)
        here = n * HALF * WIN
        sent[i] = value[:, here:]

        @pl.when(inner)
        def _():
            field_copies[i].start()

        @pl.when(jnp.logical_not(inner))
        def _():
            came[i] = sent[i]

        place(value[:, :here], w0 * WIN * PATCH, n * WIN)

    dec_load.wait()
    row_id = lax.broadcasted_iota(jnp.int32, (patches, patches), 0)
    col_id = lax.broadcasted_iota(jnp.int32, (patches, patches), 1)
    area = PATCH * PATCH
    wanted = (row_id % channels) * area + (row_id // channels) % PATCH * PATCH + row_id // part
    chosen = (col_id == wanted).astype(F32).astype(BF16)
    wdt[...] = lax.dot_general(chosen, wd[...], NT, preferred_element_type=F32).astype(BF16)

    q_id = lax.broadcasted_iota(jnp.int32, bias.shape, 0) // (HALF * WIN)
    k_id = lax.broadcasted_iota(jnp.int32, bias.shape, 1) // (HALF * WIN) % 2
    bias[...] = jnp.where((q_id != k_id) & jnp.logical_not(inner), -1e30, 0.0).astype(F32)
    eye = lax.broadcasted_iota(jnp.int32, (channels, channels), 0)
    eye = eye == lax.broadcasted_iota(jnp.int32, (channels, channels), 1)
    strength[...] = jnp.sum(jnp.where(eye, nudge_ref[...], 0.0), axis=1, keepdims=True) * undo

    strip_peer.wait_recv()
    normalize(own, edge_own, 0, windows, 0)
    query_load.wait()
    keyval_load.wait()
    project(0, windows, 0)

    state_load.wait()
    state_copy.wait_recv()
    plain_load.wait()

    @pl.loop(0, channels // LEV)
    def _(g):
        on = pl.ds(pl.multiple_of(g * LEV, LEV), LEV)
        s = band[on].reshape(LEV * tall, length)
        kept = jnp.dot(s.astype(BF16), plain[...], preferred_element_type=F32)
        kept = s.reshape(LEV, tall, length) - strength[on][:, :, None] * kept.reshape(LEV, tall, length)
        base[:, on, :] = jnp.swapaxes(kept, 0, 1)

    out_load.wait()

    @pl.when(inner)
    def _():
        strip_mate.wait_recv()

    for i, (w0, w1) in enumerate(chunks):
        token_copies[i].wait_recv()
        normalize(halo, edge_halo, w0, w1, HALF * WIN)
        project(w0, w1, HALF * WIN)
        attend(w0, w1)
        decode(i)

    patch_load.wait()
    for i, (w0, w1) in enumerate(chunks):
        n = (w1 - w0) * WIN
        last = i == count - 1
        at = wide + w0 * WIN * PATCH
        if last:
            for lane in range(0, length, 256):
                kept = jnp.dot(held[:, 0:at], patch[0:at, lane : lane + 256], preferred_element_type=F32)
                kept = strength[...][None] * kept.reshape(tall, channels, 256)
                base[:, :, lane : lane + 256] = base[:, :, lane : lane + 256] + kept

        @pl.when(inner)
        def _():
            field_copies[i].wait_recv()

        place(came[i], at, n)

    last_at = wide + chunks[-1][0] * WIN * PATCH

    def nudge_rows(r0, r1):
        kept = jnp.dot(held[r0 * part : r1 * part, last_at:], patch[last_at:, :], preferred_element_type=F32)
        y0, y1 = r0 * PATCH, r1 * PATCH
        base[y0:y1] = base[y0:y1] + strength[...][None] * kept.reshape(y1 - y0, channels, length)

    def turned(value):
        return jnp.concatenate([value[..., wide:], value[..., :wide]], axis=-1).astype(BF16)

    up_to = {"lat": jnp.where(is_low, lat, nxt), "lon": peer}
    down_to = {"lat": jnp.where(is_low, prev, lat), "lon": peer}
    inside_up, inside_down = is_low | has_next, jnp.logical_not(is_low) | has_prev
    up_copy = remote(up_copy_id, up_rows, before, up_to)
    down_copy = remote(down_copy_id, down_rows, after, down_to)
    nudge_rows(HALF - 1, HALF)
    up_rows[...] = turned(base[tall - 2 : tall])

    @pl.when(inside_up)
    def _():
        up_copy.start()

    nudge_rows(0, 1)
    down_rows[...] = turned(base[0:2])

    @pl.when(inside_down)
    def _():
        down_copy.start()

    nudge_rows(1, HALF - 1)

    def row(y):
        if y < 0:
            return before[y + 2].astype(F32)
        if y >= tall:
            return after[y - tall].astype(F32)
        return base[y]

    def section(y):
        first[y + 1] = row(y) + time_step * tendency_row(row(y - 1), row(y), row(y + 1))

    @pl.loop(1, tall - 1, unroll=7)
    def _(y):
        first[y + 1] = base[y] + time_step * tendency_row(base[y - 1], base[y], base[y + 1])

    @pl.when(inside_down)
    def _():
        up_copy.wait_recv()

    @pl.when(jnp.logical_not(inside_down))
    def _():
        before[...] = jnp.zeros_like(before)

    @pl.when(inside_up)
    def _():
        down_copy.wait_recv()

    @pl.when(jnp.logical_not(inside_up))
    def _():
        after[...] = jnp.zeros_like(after)

    for y in (-1, 0, tall - 1, tall):
        section(y)
    first[0] = first[0] * jnp.where(inside_down, 1.0, 0.0)
    first[tall + 1] = first[tall + 1] * jnp.where(inside_up, 1.0, 0.0)

    @pl.loop(0, tall, unroll=4)
    def _(y):
        second = tendency_row(first[y], first[y + 1], first[y + 2])
        base[y] = 0.5 * (base[y] + first[y + 1] + time_step * second)

    here = pl.ds(pl.multiple_of(lon * wide, 128), wide)
    there = pl.ds(pl.multiple_of(peer * wide, 128), wide)
    for g in range(0, tall, 8):
        out_ref[:, g : g + 8, here] = jnp.swapaxes(base[g : g + 8, :, 0:wide], 0, 1)
        out_ref[:, g : g + 8, there] = jnp.swapaxes(base[g : g + 8, :, wide:], 0, 1)

    for item in token_copies:
        item.wait_send()
    strip_peer.wait_send()
    state_copy.wait_send()

    @pl.when(inner)
    def _():
        strip_mate.wait_send()
        for item in field_copies:
            item.wait_send()

    @pl.when(inside_up)
    def _():
        up_copy.wait_send()

    @pl.when(inside_down)
    def _():
        down_copy.wait_send()


def body(sizes, tokens, ln_gain, w_query, w_keyval, w_out, w_dec, nudge, state):
    cols, width = tokens.shape[1:]
    channels = nudge.shape[0]
    length = state.shape[2] * sizes["lon"]
    tall = state.shape[1] // sizes["lon"]
    windows = cols // WIN
    patches = w_dec.shape[1]
    strip = 16
    chunks = chunk_bounds(windows)
    most = max(w1 - w0 for w0, w1 in chunks)
    count = len(chunks)
    cells = 2 * HALF * WIN
    hbm, vmem = pl.BlockSpec(memory_space=pl.ANY), pl.BlockSpec(memory_space=pltpu.VMEM)
    V = pltpu.VMEM
    edge_rows = V((2, channels, length), BF16)
    pieces = V((count, patches, most * HALF * WIN), BF16)
    scratch = [
        V((width, 3 * width), BF16), V((width, width), BF16), V(w_dec.shape, BF16), V((patches, width), BF16),
        V((length, length), BF16), V((length, length), BF16),
        V((HALF, cols, width), BF16), V((HALF, cols, width), BF16), V((HALF, strip, width), BF16),
        V((HALF * HALF, width), BF16), V((HALF * HALF, width), BF16),
        V((HALF * HALF, width), BF16), V((HALF * HALF, width), BF16),
        V((windows, cells, width), F32), V((windows, HALF * WIN, width), F32),
        V((windows, cells, 3 * width), BF16), V((windows, cells, width), BF16), V((most * cells, width), BF16),
        V((cells, 2 * width // HEADS), F32),
        V((channels, tall, length), F32), V((tall, channels, length), F32),
        pieces, pieces, V((HALF * PATCH * channels, length), BF16),
        edge_rows, edge_rows, edge_rows, edge_rows,
        V((tall + 2, channels, length), F32), V((channels, 1), F32),
        pltpu.SemaphoreType.DMA((9,)), pltpu.SemaphoreType.DMA((2 * count + 5,)),
        pltpu.SemaphoreType.DMA((2 * count + 5,)),
    ]
    plain, patch, undo = filter_tables(length, KEEP, windows)
    advanced = pl.pallas_call(
        functools.partial(cycle_kernel, sizes["lat"], undo),
        out_shape=jax.ShapeDtypeStruct((channels, tall, length), F32),
        in_specs=[hbm] * 8 + [vmem] * 2,
        out_specs=vmem,
        scratch_shapes=scratch,
        compiler_params=pltpu.CompilerParams(
            collective_id=0, has_side_effects=True, vmem_limit_bytes=62 * 2**20
        ),
        name="cycle",
    )(tokens, state, w_query, w_keyval, w_out, w_dec, jnp.asarray(plain), jnp.asarray(patch), ln_gain[None], nudge[None])
    return advanced


def solution(mesh):
    in_specs = (
        P(("member", "lat"), "lon", None),
        P(),
        P(),
        P(),
        P(),
        P(),
        P(),
        P(None, ("member", "lat"), "lon"),
    )
    out_specs = P(None, ("member", "lat", "lon"), None)
    return jax.shard_map(
        functools.partial(body, dict(mesh.shape)),
        mesh=mesh,
        in_specs=in_specs,
        out_specs=out_specs,
        check_vma=False,
    )
```

```python
import functools
import math

import jax
import jax.numpy as jnp
import ml_dtypes
import numpy as np
from jax import lax
from jax.experimental import pallas as pl
from jax.experimental.pallas import tpu as pltpu
from jax.sharding import PartitionSpec as P

HEADS = 16
WIN = 8
PATCH = 4
VARS = 4
LEV = 8
KEEP = 256

time_step = 0.1
diffusion = 0.5
epsilon = 1e-05
F32 = jnp.float32
BF16 = jnp.bfloat16
NT = (((1,), (1,)), ((), ()))
HALF = WIN // 2
MESH = pl.DeviceIdType.MESH


def chunk_bounds(windows):
    size = 4
    return [(w, min(w + size, windows)) for w in range(0, windows, size)]


def filter_tables(length, kept, windows):
    offset = np.arange(length)
    waves = np.arange(1, kept)
    angles = 2.0 * np.pi * ((offset[:, None] * waves[None, :]) % length) / length
    kernel = (1.0 + 2.0 * np.cos(angles).sum(1)) / length
    pixel = []
    for side in range(2):
        for w0, w1 in chunk_bounds(windows):
            for b in range(PATCH):
                column = np.arange(w0 * WIN, w1 * WIN) + HALF
                pixel.append(side * (length // 2) + PATCH * column + b)
    pixel = np.concatenate(pixel)
    plain = (offset[None, :] - offset[:, None]) % length
    patch = (offset[None, :] - pixel[:, None]) % length

    def rounded(factor):
        return (kernel * factor).astype(np.float32).astype(ml_dtypes.bfloat16)

    factors = 1.0 + np.arange(2048) / 2048
    errors = [np.square(rounded(f).astype(np.float64) / f - kernel).sum() for f in factors]
    factor = float(factors[int(np.argmin(errors))])
    return rounded(factor)[plain], rounded(factor)[patch], 1.0 / factor


def tendency_row(south, centre, north):
    channels, length = centre.shape
    west = pltpu.roll(centre, 1, 1)
    east = pltpu.roll(centre, length - 1, 1)
    u = centre[:LEV][None]
    v = centre[LEV : 2 * LEV][None]
    dx = (east - west).reshape(VARS, LEV, length)
    dy = (north - south).reshape(VARS, LEV, length)
    advection = ((u * dx + v * dy) * 0.5).reshape(channels, length)
    return diffusion * (east + west + north + south - 4.0 * centre) - advection


def cycle_kernel(
    n_lat, undo, tokens, state, wq_hbm, wkv_hbm, wo_hbm, wd_hbm, plain_hbm, patch_hbm, gain_ref, nudge_ref, base, first,
    wqkv, wo, wd, wdt, plain, patch, own, halo, side, strip_own, strip_far, edge_own, edge_halo,
    xs, normed, qkv, att, lo, bias, band, sent, came, held, up_rows, down_rows, before, after, strength,
    load_sem, send_sem, recv_sem, credit,
):
    lat, lon = lax.axis_index("lat"), lax.axis_index("lon")
    peer = 1 - lon
    cols, width = tokens.shape[1:]
    windows = cols // WIN
    cells = 2 * HALF * WIN
    tall, channels, length = base.shape
    wide = length // 2
    chunks = chunk_bounds(windows)
    count = len(chunks)
    is_low = lon == 0
    has_prev, has_next = lat > 0, lat < n_lat - 1
    prev, nxt = jnp.maximum(lat - 1, 0), jnp.minimum(lat + 1, n_lat - 1)
    inner = jnp.where(is_low, has_prev, has_next)
    more = jnp.where(is_low, has_next, has_prev)
    ring = {"lat": jnp.where(is_low, nxt, prev), "lon": jnp.where(more, lon, peer)}
    mate = {"lat": jnp.where(is_low, prev, nxt), "lon": peer}
    side_by = {"lat": lat, "lon": peer}

    def load(i, src, dst):
        return pltpu.make_async_copy(src, dst, load_sem.at[i])

    def remote(i, src, dst, to):
        return pltpu.make_async_remote_copy(
            src_ref=src, dst_ref=dst, send_sem=send_sem.at[i], recv_sem=recv_sem.at[i],
            device_id=to, device_id_type=MESH,
        )

    own_at = pl.multiple_of(lon * HALF, HALF)
    far_at = pl.multiple_of(peer * HALF, HALF)
    strip = side.shape[1]
    side_load = load(0, tokens.at[pl.ds(far_at, HALF), pl.ds(0, strip), :], side)
    own_load = load(1, tokens.at[pl.ds(own_at, HALF)], own)
    dec_load = load(2, wd_hbm, wd)
    query_load = load(3, wq_hbm, wqkv.at[:, pl.ds(0, width)])
    keyval_load = load(4, wkv_hbm, wqkv.at[:, pl.ds(width, 2 * width)])
    my_rows = pl.ds(pl.multiple_of(lon * tall, 8), tall)
    peer_rows = pl.ds(pl.multiple_of(peer * tall, 8), tall)
    state_load = load(5, state.at[:, my_rows, :], band.at[:, :, pl.ds(0, wide)])
    plain_load = load(6, plain_hbm, plain)
    out_load = load(7, wo_hbm, wo)
    patch_load = load(8, patch_hbm, patch)
    side_load.start()
    own_load.start()

    barrier = pltpu.get_barrier_semaphore()

    def greet(to):
        pl.semaphore_signal(barrier, inc=1, device_id=to, device_id_type=MESH)

    greet(side_by)

    @pl.when(has_prev)
    def _():
        greet({"lat": prev, "lon": lon})

    @pl.when(has_next)
    def _():
        greet({"lat": nxt, "lon": lon})

    @pl.when(inner)
    def _():
        greet(mate)

    pl.semaphore_wait(
        barrier, 1 + has_prev.astype(jnp.int32) + has_next.astype(jnp.int32) + inner.astype(jnp.int32)
    )

    ends = [min(cols, -(-(w1 * WIN + HALF) // strip) * strip) for _, w1 in chunks]
    token_copies = []
    for i, (begin, end) in enumerate(zip([0] + ends[:-1], ends)):
        at = pl.ds(begin, end - begin)
        token_copies.append(remote(i, tokens.at[pl.ds(far_at, HALF), at, :], halo.at[:, at, :], ring))
    token_copies[0].start()
    for item in (dec_load, query_load, keyval_load, state_load, plain_load, out_load, patch_load):
        item.start()
    base_id = count
    state_copy = remote(base_id, state.at[:, peer_rows, :], band.at[:, :, pl.ds(wide, wide)], side_by)
    strip_peer = remote(base_id + 1, strip_far, edge_own, side_by)
    strip_mate = remote(base_id + 2, strip_own, edge_halo, mate)
    field_copies = [remote(base_id + 3 + i, sent.at[i], came.at[i], mate) for i in range(count)]
    up_copy_id, down_copy_id = base_id + 3 + count, base_id + 4 + count

    def pack(source, out):
        for r in range(0, HALF, 2):
            pair = [source[r + j, 0:WIN, :].astype(F32)[:HALF] for j in range(2)]
            out[r * HALF : (r + 2) * HALF, :] = jnp.concatenate(pair, axis=0).astype(BF16)

    side_load.wait()
    pack(side, strip_far)
    strip_peer.start()
    own_load.wait()
    pack(own, strip_own)

    @pl.when(inner)
    def _():
        strip_mate.start()

    @pl.when(jnp.logical_not(inner))
    def _():
        edge_halo[...] = strip_own[...]

    state_copy.start()

    def normalize(source, edge, w0, w1, at):
        c0, c1 = w0 * WIN, w1 * WIN
        n = w1 - w0
        for r in range(HALF):
            if c1 < cols:
                block = source[r, c0 : c1 + WIN, :].astype(F32)[HALF : HALF + n * WIN]
            else:
                block = source[r, c0:c1, :].astype(F32)[HALF:]
                r0 = r // 2 * WIN
                tail = edge[r0 : r0 + WIN, :].astype(F32)[r % 2 * HALF : r % 2 * HALF + HALF]
                block = jnp.concatenate([block, tail], axis=0)
            centred = block - jnp.mean(block, axis=-1, keepdims=True)
            variance = jnp.mean(centred * centred, axis=-1, keepdims=True)
            unit = centred * lax.rsqrt(variance + epsilon) * gain_ref[...]
            xs[w0:w1, at + r * WIN : at + (r + 1) * WIN, :] = block.reshape(n, WIN, width)
            normed[w0:w1, r * WIN : (r + 1) * WIN, :] = unit.reshape(n, WIN, width)

    scale = math.log2(math.e) / math.sqrt(width // HEADS)

    def project(w0, w1, at):
        n = w1 - w0
        flat = normed[w0:w1].reshape(n * HALF * WIN, width).astype(BF16)
        for part in range(3):
            on = slice(part * width, (part + 1) * width)
            value = jnp.dot(flat, wqkv[:, on], preferred_element_type=F32)
            if part == 0:
                value = value * scale
            qkv[w0:w1, at : at + HALF * WIN, on] = value.astype(BF16).reshape(n, HALF * WIN, width)

    def attend(w0, w1):
        head = width // HEADS
        pair = 2 * head
        lanes = lax.broadcasted_iota(jnp.int32, (cells, pair), 1) < head
        left = lax.broadcasted_iota(jnp.int32, (2 * cells, pair), 1) < head
        upper = lax.broadcasted_iota(jnp.int32, (2 * cells, pair), 0) < cells
        ones = (left == upper).astype(F32).astype(BF16)

        def both(x):
            zero = jnp.zeros_like(x)
            return jnp.concatenate([jnp.where(lanes, x, zero), jnp.where(lanes, zero, x)], axis=0)

        @pl.loop(w0, w1, unroll=w1 - w0)
        def _(w):
            spots = [p * pair for p in range(HEADS // 2)]
            scores = []
            for on in spots:
                q = qkv[w, :, on : on + pair]
                k = both(qkv[w, :, width + on : width + on + pair])
                scores.append(lax.dot_general(q, k, NT, preferred_element_type=F32) + bias[...])
            powers = []
            for s in scores:
                low = jnp.max(jnp.where(lanes, s, -jnp.inf), axis=-1, keepdims=True)
                high = jnp.max(jnp.where(lanes, -jnp.inf, s), axis=-1, keepdims=True)
                powers.append(jnp.exp2(s - jnp.where(lanes, low, high)).astype(BF16))
            mixed = []
            for on, e in zip(spots, powers):
                v = both(qkv[w, :, 2 * width + on : 2 * width + on + pair])
                o = jnp.dot(e, jnp.concatenate([v, ones], axis=1), preferred_element_type=F32)
                mixed.append((o[:, :pair] / o[:, pair:]).astype(BF16))
            att[w] = jnp.concatenate(mixed, axis=1)

    patches = wdt.shape[0]
    part = PATCH * channels

    def place(value, at, n):
        for r in range(HALF):
            pieces = [value[b * part : (b + 1) * part, r * n : (r + 1) * n] for b in range(PATCH)]
            held[r * part : (r + 1) * part, at : at + PATCH * n] = jnp.concatenate(pieces, axis=1)

    def decode(i):
        w0, w1 = chunks[i]
        n = w1 - w0
        mixed = att[w0:w1].reshape(n * cells, width)
        for at in range(0, width, 512):
            update = jnp.dot(mixed, wo[:, at : at + 512], preferred_element_type=F32)
            value = xs[w0:w1, :, at : at + 512] + update.reshape(n, cells, 512)
            value = value.reshape(n, 2 * HALF, WIN, 512)
            value = jnp.swapaxes(value, 0, 1).reshape(n * cells, 512)
            lo[0 : n * cells, at : at + 512] = value.astype(BF16)
        value = lax.dot_general(wdt[...], lo[0 : n * cells, :], NT, preferred_element_type=F32).astype(BF16)
        here = n * HALF * WIN
        sent[i] = value[:, here:]

        @pl.when(jnp.logical_not(inner))
        def _():
            came[i] = sent[i]

        place(value[:, :here], w0 * WIN * PATCH, n * WIN)

    dec_load.wait()
    row_id = lax.broadcasted_iota(jnp.int32, (patches, patches), 0)
    col_id = lax.broadcasted_iota(jnp.int32, (patches, patches), 1)
    area = PATCH * PATCH
    wanted = (row_id % channels) * area + (row_id // channels) % PATCH * PATCH + row_id // part
    chosen = (col_id == wanted).astype(F32).astype(BF16)
    wdt[...] = lax.dot_general(chosen, wd[...], NT, preferred_element_type=F32).astype(BF16)

    q_id = lax.broadcasted_iota(jnp.int32, bias.shape, 0) // (HALF * WIN)
    k_id = lax.broadcasted_iota(jnp.int32, bias.shape, 1) // (HALF * WIN) % 2
    bias[...] = jnp.where((q_id != k_id) & jnp.logical_not(inner), -1e30, 0.0).astype(F32)
    eye = lax.broadcasted_iota(jnp.int32, (channels, channels), 0)
    eye = eye == lax.broadcasted_iota(jnp.int32, (channels, channels), 1)
    strength[...] = jnp.sum(jnp.where(eye, nudge_ref[...], 0.0), axis=1, keepdims=True) * undo

    strip_peer.wait_recv()
    normalize(own, edge_own, 0, windows, 0)
    query_load.wait()
    keyval_load.wait()
    project(0, windows, 0)

    state_load.wait()
    state_copy.wait_recv()
    plain_load.wait()

    @pl.loop(0, channels // LEV)
    def _(g):
        on = pl.ds(pl.multiple_of(g * LEV, LEV), LEV)
        s = band[on].reshape(LEV * tall, length)
        kept = jnp.dot(s.astype(BF16), plain[...], preferred_element_type=F32)
        kept = s.reshape(LEV, tall, length) - strength[on][:, :, None] * kept.reshape(LEV, tall, length)
        base[:, on, :] = jnp.swapaxes(kept, 0, 1)

    out_load.wait()

    @pl.when(inner)
    def _():
        strip_mate.wait_recv()

    def follow(i):
        if i < count - 1:
            token_copies[i + 1].start()

    token_copies[0].wait_recv()
    follow(0)
    for i, (w0, w1) in enumerate(chunks):
        normalize(halo, edge_halo, w0, w1, HALF * WIN)
        project(w0, w1, HALF * WIN)
        attend(w0, w1)
        if i < count - 1:
            follow(i + 1)
            token_copies[i + 1].wait_recv()
        if i == count - 2:

            pass

        decode(i)
        @pl.when(inner)
        def _():
            field_copies[i].start()

    patch_load.wait()
    for i, (w0, w1) in enumerate(chunks):
        n = (w1 - w0) * WIN
        last = i == count - 1
        at = wide + w0 * WIN * PATCH
        if last:
            for lane in range(0, length, 256):
                kept = jnp.dot(held[:, 0:at], patch[0:at, lane : lane + 256], preferred_element_type=F32)
                kept = strength[...][None] * kept.reshape(tall, channels, 256)
                base[:, :, lane : lane + 256] = base[:, :, lane : lane + 256] + kept

        @pl.when(inner)
        def _():
            field_copies[i].wait_recv()

        place(came[i], at, n)

    last_at = wide + chunks[-1][0] * WIN * PATCH

    def nudge_rows(r0, r1):
        kept = jnp.dot(held[r0 * part : r1 * part, last_at:], patch[last_at:, :], preferred_element_type=F32)
        y0, y1 = r0 * PATCH, r1 * PATCH
        base[y0:y1] = base[y0:y1] + strength[...][None] * kept.reshape(y1 - y0, channels, length)

    def turned(value):
        return jnp.concatenate([value[..., wide:], value[..., :wide]], axis=-1).astype(BF16)

    up_to = {"lat": jnp.where(is_low, lat, nxt), "lon": peer}
    down_to = {"lat": jnp.where(is_low, prev, lat), "lon": peer}
    inside_up, inside_down = is_low | has_next, jnp.logical_not(is_low) | has_prev
    up_copy = remote(up_copy_id, up_rows, before, up_to)
    down_copy = remote(down_copy_id, down_rows, after, down_to)
    nudge_rows(HALF - 1, HALF)
    up_rows[...] = turned(base[tall - 2 : tall])

    @pl.when(inside_up)
    def _():
        up_copy.start()

    nudge_rows(0, 1)
    down_rows[...] = turned(base[0:2])

    @pl.when(inside_down)
    def _():
        down_copy.start()

    nudge_rows(1, HALF - 1)

    def row(y):
        if y < 0:
            return before[y + 2].astype(F32)
        if y >= tall:
            return after[y - tall].astype(F32)
        return base[y]

    def section(y):
        first[y + 1] = row(y) + time_step * tendency_row(row(y - 1), row(y), row(y + 1))

    @pl.loop(1, tall - 1, unroll=7)
    def _(y):
        first[y + 1] = base[y] + time_step * tendency_row(base[y - 1], base[y], base[y + 1])

    @pl.when(inside_down)
    def _():
        up_copy.wait_recv()

    @pl.when(jnp.logical_not(inside_down))
    def _():
        before[...] = jnp.zeros_like(before)

    @pl.when(inside_up)
    def _():
        down_copy.wait_recv()

    @pl.when(jnp.logical_not(inside_up))
    def _():
        after[...] = jnp.zeros_like(after)

    for y in (-1, 0, tall - 1, tall):
        section(y)
    first[0] = first[0] * jnp.where(inside_down, 1.0, 0.0)
    first[tall + 1] = first[tall + 1] * jnp.where(inside_up, 1.0, 0.0)

    for item in token_copies:
        item.wait_send()
    strip_peer.wait_send()
    state_copy.wait_send()

    @pl.when(inner)
    def _():
        strip_mate.wait_send()
        for item in field_copies:
            item.wait_send()

    @pl.when(inside_up)
    def _():
        up_copy.wait_send()

    @pl.when(inside_down)
    def _():
        down_copy.wait_send()


def second_kernel(base, first, out_ref):
    tall, channels, length = base.shape
    wide = length // 2
    lon = lax.axis_index("lon")
    here = pl.ds(pl.multiple_of(lon * wide, 128), wide)
    there = pl.ds(pl.multiple_of((1 - lon) * wide, 128), wide)
    for g in range(0, tall, 8):
        rows = []
        for y in range(g, g + 8):
            second = tendency_row(first[y], first[y + 1], first[y + 2])
            rows.append(0.5 * (base[y] + first[y + 1] + time_step * second))
        value = jnp.swapaxes(jnp.stack(rows), 0, 1)
        out_ref[:, g : g + 8, here] = value[:, :, 0:wide]
        out_ref[:, g : g + 8, there] = value[:, :, wide:]


def body(sizes, tokens, ln_gain, w_query, w_keyval, w_out, w_dec, nudge, state):
    cols, width = tokens.shape[1:]
    channels = nudge.shape[0]
    length = state.shape[2] * sizes["lon"]
    tall = state.shape[1] // sizes["lon"]
    windows = cols // WIN
    patches = w_dec.shape[1]
    strip = 16
    chunks = chunk_bounds(windows)
    most = max(w1 - w0 for w0, w1 in chunks)
    count = len(chunks)
    cells = 2 * HALF * WIN
    hbm, vmem = pl.BlockSpec(memory_space=pl.ANY), pl.BlockSpec(memory_space=pltpu.VMEM)
    V = pltpu.VMEM
    edge_rows = V((2, channels, length), BF16)
    pieces = V((count, patches, most * HALF * WIN), BF16)
    scratch = [
        V((width, 3 * width), BF16), V((width, width), BF16), V(w_dec.shape, BF16), V((patches, width), BF16),
        V((length, length), BF16), V((length, length), BF16),
        V((HALF, cols, width), BF16), V((HALF, cols, width), BF16), V((HALF, strip, width), BF16),
        V((HALF * HALF, width), BF16), V((HALF * HALF, width), BF16),
        V((HALF * HALF, width), BF16), V((HALF * HALF, width), BF16),
        V((windows, cells, width), F32), V((windows, HALF * WIN, width), F32),
        V((windows, cells, 3 * width), BF16), V((windows, cells, width), BF16), V((most * cells, width), BF16),
        V((cells, 2 * width // HEADS), F32),
        V((channels, tall, length), F32),
        pieces, pieces, V((HALF * PATCH * channels, length), BF16),
        edge_rows, edge_rows, edge_rows, edge_rows,
        V((channels, 1), F32),
        pltpu.SemaphoreType.DMA((9,)), pltpu.SemaphoreType.DMA((2 * count + 5,)),
        pltpu.SemaphoreType.DMA((2 * count + 5,)), pltpu.SemaphoreType.REGULAR,
    ]
    plain, patch, undo = filter_tables(length, KEEP, windows)
    nudged, first = pl.pallas_call(
        functools.partial(cycle_kernel, sizes["lat"], undo),
        out_shape=[
            pltpu.VMEM((tall, channels, length), F32),
            pltpu.VMEM((tall + 2, channels, length), F32),
        ],
        in_specs=[hbm] * 8 + [vmem] * 2,
        out_specs=[vmem, vmem],
        scratch_shapes=scratch,
        compiler_params=pltpu.CompilerParams(
            collective_id=0, has_side_effects=True, vmem_limit_bytes=56 * 2**20
        ),
        name="cycle",
    )(tokens, state, w_query, w_keyval, w_out, w_dec, jnp.asarray(plain), jnp.asarray(patch), ln_gain[None], nudge[None])
    return pl.pallas_call(
        second_kernel,
        out_shape=jax.ShapeDtypeStruct((channels, tall, length), F32),
        in_specs=[vmem, vmem],
        out_specs=vmem,
        compiler_params=pltpu.CompilerParams(vmem_limit_bytes=16 * 2**20),
        name="second",
    )(nudged, first)


def solution(mesh):
    in_specs = (
        P(("member", "lat"), "lon", None),
        P(),
        P(),
        P(),
        P(),
        P(),
        P(),
        P(None, ("member", "lat"), "lon"),
    )
    out_specs = P(None, ("member", "lat", "lon"), None)
    return jax.shard_map(
        functools.partial(body, dict(mesh.shape)),
        mesh=mesh,
        in_specs=in_specs,
        out_specs=out_specs,
        check_vma=False,
    )
```

```python
import functools
import math

import jax
import jax.numpy as jnp
import ml_dtypes
import numpy as np
from jax import lax
from jax.experimental import pallas as pl
from jax.experimental.pallas import tpu as pltpu
from jax.sharding import PartitionSpec as P

HEADS = 16
WIN = 8
PATCH = 4
VARS = 4
LEV = 8
KEEP = 256

time_step = 0.1
diffusion = 0.5
epsilon = 1e-05
F32 = jnp.float32
BF16 = jnp.bfloat16
NT = (((1,), (1,)), ((), ()))
HALF = WIN // 2
MESH = pl.DeviceIdType.MESH


def chunk_bounds(windows):
    size = 4
    return [(w, min(w + size, windows)) for w in range(0, windows, size)]


def filter_tables(length, kept, windows):
    offset = np.arange(length)
    waves = np.arange(1, kept)
    angles = 2.0 * np.pi * ((offset[:, None] * waves[None, :]) % length) / length
    kernel = (1.0 + 2.0 * np.cos(angles).sum(1)) / length
    pixel = []
    for side in range(2):
        for w0, w1 in chunk_bounds(windows):
            for b in range(PATCH):
                column = np.arange(w0 * WIN, w1 * WIN) + HALF
                pixel.append(side * (length // 2) + PATCH * column + b)
    pixel = np.concatenate(pixel)
    plain = (offset[None, :] - offset[:, None]) % length
    patch = (offset[None, :] - pixel[:, None]) % length

    def rounded(factor):
        return (kernel * factor).astype(np.float32).astype(ml_dtypes.bfloat16)

    factors = 1.0 + np.arange(2048) / 2048
    errors = [np.square(rounded(f).astype(np.float64) / f - kernel).sum() for f in factors]
    factor = float(factors[int(np.argmin(errors))])
    return rounded(factor)[plain], rounded(factor)[patch], 1.0 / factor


def tendency_row(south, centre, north):
    channels, length = centre.shape
    west = pltpu.roll(centre, 1, 1)
    east = pltpu.roll(centre, length - 1, 1)
    u = centre[:LEV][None]
    v = centre[LEV : 2 * LEV][None]
    dx = (east - west).reshape(VARS, LEV, length)
    dy = (north - south).reshape(VARS, LEV, length)
    advection = ((u * dx + v * dy) * 0.5).reshape(channels, length)
    return diffusion * (east + west + north + south - 4.0 * centre) - advection


def cycle_kernel(
    n_lat, undo, tokens, state, wq_hbm, wkv_hbm, wo_hbm, wd_hbm, plain_hbm, patch_hbm, gain_ref, nudge_ref, base, first,
    wqkv, wo, wd, wdt, plain, patch, own, halo, side, strip_own, strip_far, edge_own, edge_halo,
    xs, normed, qkv, att, lo, bias, band, sent, came, held, up_rows, down_rows, before, after, strength,
    load_sem, send_sem, recv_sem,
):
    lat, lon = lax.axis_index("lat"), lax.axis_index("lon")
    peer = 1 - lon
    cols, width = tokens.shape[1:]
    windows = cols // WIN
    cells = 2 * HALF * WIN
    tall, channels, length = base.shape
    wide = length // 2
    chunks = chunk_bounds(windows)
    count = len(chunks)
    is_low = lon == 0
    has_prev, has_next = lat > 0, lat < n_lat - 1
    prev, nxt = jnp.maximum(lat - 1, 0), jnp.minimum(lat + 1, n_lat - 1)
    inner = jnp.where(is_low, has_prev, has_next)
    more = jnp.where(is_low, has_next, has_prev)
    ring = {"lat": jnp.where(is_low, nxt, prev), "lon": jnp.where(more, lon, peer)}
    mate = {"lat": jnp.where(is_low, prev, nxt), "lon": peer}
    side_by = {"lat": lat, "lon": peer}

    def load(i, src, dst):
        return pltpu.make_async_copy(src, dst, load_sem.at[i])

    def remote(i, src, dst, to):
        return pltpu.make_async_remote_copy(
            src_ref=src, dst_ref=dst, send_sem=send_sem.at[i], recv_sem=recv_sem.at[i],
            device_id=to, device_id_type=MESH,
        )

    own_at = pl.multiple_of(lon * HALF, HALF)
    far_at = pl.multiple_of(peer * HALF, HALF)
    strip = side.shape[1]
    side_load = load(0, tokens.at[pl.ds(far_at, HALF), pl.ds(0, strip), :], side)
    own_load = load(1, tokens.at[pl.ds(own_at, HALF)], own)
    dec_load = load(2, wd_hbm, wd)
    query_load = load(3, wq_hbm, wqkv.at[:, pl.ds(0, width)])
    keyval_load = load(4, wkv_hbm, wqkv.at[:, pl.ds(width, 2 * width)])
    my_rows = pl.ds(pl.multiple_of(lon * tall, 8), tall)
    peer_rows = pl.ds(pl.multiple_of(peer * tall, 8), tall)
    state_load = load(5, state.at[:, my_rows, :], band.at[:, :, pl.ds(0, wide)])
    plain_load = load(6, plain_hbm, plain)
    out_load = load(7, wo_hbm, wo)
    patch_load = load(8, patch_hbm, patch)
    side_load.start()
    own_load.start()

    barrier = pltpu.get_barrier_semaphore()

    def greet(to):
        pl.semaphore_signal(barrier, inc=1, device_id=to, device_id_type=MESH)

    greet(side_by)

    @pl.when(has_prev)
    def _():
        greet({"lat": prev, "lon": lon})

    @pl.when(has_next)
    def _():
        greet({"lat": nxt, "lon": lon})

    @pl.when(inner)
    def _():
        greet(mate)

    pl.semaphore_wait(
        barrier, 1 + has_prev.astype(jnp.int32) + has_next.astype(jnp.int32) + inner.astype(jnp.int32)
    )

    ends = [min(cols, -(-(w1 * WIN + HALF) // strip) * strip) for _, w1 in chunks]
    token_copies = []
    for i, (begin, end) in enumerate(zip([0] + ends[:-1], ends)):
        at = pl.ds(begin, end - begin)
        token_copies.append(remote(i, tokens.at[pl.ds(far_at, HALF), at, :], halo.at[:, at, :], ring))
    token_copies[0].start()
    for item in (dec_load, query_load, keyval_load, state_load, plain_load, out_load, patch_load):
        item.start()
    base_id = count
    state_copy = remote(base_id, state.at[:, peer_rows, :], band.at[:, :, pl.ds(wide, wide)], side_by)
    strip_peer = remote(base_id + 1, strip_far, edge_own, side_by)
    strip_mate = remote(base_id + 2, strip_own, edge_halo, mate)
    field_copies = [remote(base_id + 3 + i, sent.at[i], came.at[i], mate) for i in range(count)]
    up_copy_id, down_copy_id = base_id + 3 + count, base_id + 4 + count

    def pack(source, out):
        for r in range(0, HALF, 2):
            pair = [source[r + j, 0:WIN, :].astype(F32)[:HALF] for j in range(2)]
            out[r * HALF : (r + 2) * HALF, :] = jnp.concatenate(pair, axis=0).astype(BF16)

    side_load.wait()
    pack(side, strip_far)
    strip_peer.start()
    own_load.wait()
    pack(own, strip_own)

    @pl.when(inner)
    def _():
        strip_mate.start()

    @pl.when(jnp.logical_not(inner))
    def _():
        edge_halo[...] = strip_own[...]

    state_copy.start()

    def normalize(source, edge, w0, w1, at):
        c0, c1 = w0 * WIN, w1 * WIN
        n = w1 - w0
        for r in range(HALF):
            if c1 < cols:
                block = source[r, c0 : c1 + WIN, :].astype(F32)[HALF : HALF + n * WIN]
            else:
                block = source[r, c0:c1, :].astype(F32)[HALF:]
                r0 = r // 2 * WIN
                tail = edge[r0 : r0 + WIN, :].astype(F32)[r % 2 * HALF : r % 2 * HALF + HALF]
                block = jnp.concatenate([block, tail], axis=0)
            centred = block - jnp.mean(block, axis=-1, keepdims=True)
            variance = jnp.mean(centred * centred, axis=-1, keepdims=True)
            unit = centred * lax.rsqrt(variance + epsilon) * gain_ref[...]
            xs[w0:w1, at + r * WIN : at + (r + 1) * WIN, :] = block.reshape(n, WIN, width)
            normed[w0:w1, r * WIN : (r + 1) * WIN, :] = unit.reshape(n, WIN, width)

    scale = math.log2(math.e) / math.sqrt(width // HEADS)

    def project(w0, w1, at):
        n = w1 - w0
        flat = normed[w0:w1].reshape(n * HALF * WIN, width).astype(BF16)
        for part in range(3):
            on = slice(part * width, (part + 1) * width)
            value = jnp.dot(flat, wqkv[:, on], preferred_element_type=F32)
            if part == 0:
                value = value * scale
            qkv[w0:w1, at : at + HALF * WIN, on] = value.astype(BF16).reshape(n, HALF * WIN, width)

    def attend(w0, w1):
        head = width // HEADS
        pair = 2 * head
        lanes = lax.broadcasted_iota(jnp.int32, (cells, pair), 1) < head
        left = lax.broadcasted_iota(jnp.int32, (2 * cells, pair), 1) < head
        upper = lax.broadcasted_iota(jnp.int32, (2 * cells, pair), 0) < cells
        ones = (left == upper).astype(F32).astype(BF16)

        def both(x):
            zero = jnp.zeros_like(x)
            return jnp.concatenate([jnp.where(lanes, x, zero), jnp.where(lanes, zero, x)], axis=0)

        @pl.loop(w0, w1, unroll=w1 - w0)
        def _(w):
            spots = [p * pair for p in range(HEADS // 2)]
            scores = []
            for on in spots:
                q = qkv[w, :, on : on + pair]
                k = both(qkv[w, :, width + on : width + on + pair])
                scores.append(lax.dot_general(q, k, NT, preferred_element_type=F32) + bias[...])
            powers = []
            for s in scores:
                low = jnp.max(jnp.where(lanes, s, -jnp.inf), axis=-1, keepdims=True)
                high = jnp.max(jnp.where(lanes, -jnp.inf, s), axis=-1, keepdims=True)
                powers.append(jnp.exp2(s - jnp.where(lanes, low, high)).astype(BF16))
            mixed = []
            for on, e in zip(spots, powers):
                v = both(qkv[w, :, 2 * width + on : 2 * width + on + pair])
                o = jnp.dot(e, jnp.concatenate([v, ones], axis=1), preferred_element_type=F32)
                mixed.append((o[:, :pair] / o[:, pair:]).astype(BF16))
            att[w] = jnp.concatenate(mixed, axis=1)

    patches = wdt.shape[0]
    part = PATCH * channels

    def place(value, at, n):
        for r in range(HALF):
            pieces = [value[b * part : (b + 1) * part, r * n : (r + 1) * n] for b in range(PATCH)]
            held[r * part : (r + 1) * part, at : at + PATCH * n] = jnp.concatenate(pieces, axis=1)

    def decode(i):
        w0, w1 = chunks[i]
        n = w1 - w0
        mixed = att[w0:w1].reshape(n * cells, width)
        for at in range(0, width, 512):
            update = jnp.dot(mixed, wo[:, at : at + 512], preferred_element_type=F32)
            value = xs[w0:w1, :, at : at + 512] + update.reshape(n, cells, 512)
            value = value.reshape(n, 2 * HALF, WIN, 512)
            value = jnp.swapaxes(value, 0, 1).reshape(n * cells, 512)
            lo[0 : n * cells, at : at + 512] = value.astype(BF16)
        value = lax.dot_general(wdt[...], lo[0 : n * cells, :], NT, preferred_element_type=F32).astype(BF16)
        here = n * HALF * WIN
        sent[i] = value[:, here:]

        @pl.when(inner)
        def _():
            field_copies[i].start()

        @pl.when(jnp.logical_not(inner))
        def _():
            came[i] = sent[i]

        place(value[:, :here], w0 * WIN * PATCH, n * WIN)

    dec_load.wait()
    row_id = lax.broadcasted_iota(jnp.int32, (patches, patches), 0)
    col_id = lax.broadcasted_iota(jnp.int32, (patches, patches), 1)
    area = PATCH * PATCH
    wanted = (row_id % channels) * area + (row_id // channels) % PATCH * PATCH + row_id // part
    chosen = (col_id == wanted).astype(F32).astype(BF16)
    wdt[...] = lax.dot_general(chosen, wd[...], NT, preferred_element_type=F32).astype(BF16)

    q_id = lax.broadcasted_iota(jnp.int32, bias.shape, 0) // (HALF * WIN)
    k_id = lax.broadcasted_iota(jnp.int32, bias.shape, 1) // (HALF * WIN) % 2
    bias[...] = jnp.where((q_id != k_id) & jnp.logical_not(inner), -1e30, 0.0).astype(F32)
    eye = lax.broadcasted_iota(jnp.int32, (channels, channels), 0)
    eye = eye == lax.broadcasted_iota(jnp.int32, (channels, channels), 1)
    strength[...] = jnp.sum(jnp.where(eye, nudge_ref[...], 0.0), axis=1, keepdims=True) * undo

    strip_peer.wait_recv()
    normalize(own, edge_own, 0, windows, 0)
    query_load.wait()
    keyval_load.wait()
    project(0, windows, 0)

    state_load.wait()
    state_copy.wait_recv()
    plain_load.wait()

    @pl.loop(0, channels // LEV)
    def _(g):
        on = pl.ds(pl.multiple_of(g * LEV, LEV), LEV)
        s = band[on].reshape(LEV * tall, length)
        kept = jnp.dot(s.astype(BF16), plain[...], preferred_element_type=F32)
        kept = s.reshape(LEV, tall, length) - strength[on][:, :, None] * kept.reshape(LEV, tall, length)
        base[:, on, :] = jnp.swapaxes(kept, 0, 1)

    out_load.wait()

    @pl.when(inner)
    def _():
        strip_mate.wait_recv()

    token_copies[0].wait_recv()
    token_copies[1].start()
    for i, (w0, w1) in enumerate(chunks):
        normalize(halo, edge_halo, w0, w1, HALF * WIN)
        project(w0, w1, HALF * WIN)
        attend(w0, w1)
        if i < count - 1:
            if i + 2 < count:
                token_copies[i + 2].start()
            token_copies[i + 1].wait_recv()
        decode(i)

    patch_load.wait()
    for i, (w0, w1) in enumerate(chunks):
        n = (w1 - w0) * WIN
        last = i == count - 1
        at = wide + w0 * WIN * PATCH
        if last:
            for lane in range(0, length, 256):
                kept = jnp.dot(held[:, 0:at], patch[0:at, lane : lane + 256], preferred_element_type=F32)
                kept = strength[...][None] * kept.reshape(tall, channels, 256)
                base[:, :, lane : lane + 256] = base[:, :, lane : lane + 256] + kept

        @pl.when(inner)
        def _():
            field_copies[i].wait_recv()

        place(came[i], at, n)

    last_at = wide + chunks[-1][0] * WIN * PATCH

    def nudge_rows(r, n):
        at, y = pl.multiple_of(r * part, part), r * PATCH
        kept = jnp.dot(held[pl.ds(at, n * part), last_at:], patch[last_at:, :], preferred_element_type=F32)
        rows = pl.ds(y, n * PATCH)
        base[rows] = base[rows] + strength[...][None] * kept.reshape(n * PATCH, channels, length)

    def turned(value):
        return jnp.concatenate([value[..., wide:], value[..., :wide]], axis=-1).astype(BF16)

    up_to = {"lat": jnp.where(is_low, lat, nxt), "lon": peer}
    down_to = {"lat": jnp.where(is_low, prev, lat), "lon": peer}
    inside_up, inside_down = is_low | has_next, jnp.logical_not(is_low) | has_prev
    up_copy = remote(up_copy_id, up_rows, before, up_to)
    down_copy = remote(down_copy_id, down_rows, after, down_to)

    def send_up():
        up_rows[...] = turned(base[tall - 2 : tall])
        up_copy.start()

    def send_down():
        down_rows[...] = turned(base[0:2])
        down_copy.start()

    nudge_rows(jnp.where(is_low, 0, HALF - 1), 1)
    pl.when(is_low & has_prev)(send_down)
    pl.when(jnp.logical_not(is_low) & has_next)(send_up)
    nudge_rows(jnp.where(is_low, HALF - 1, 0), 1)
    pl.when(is_low)(send_up)
    pl.when(jnp.logical_not(is_low))(send_down)
    nudge_rows(1, HALF - 2)

    def row(y):
        if y < 0:
            return before[y + 2].astype(F32)
        if y >= tall:
            return after[y - tall].astype(F32)
        return base[y]

    def section(y):
        first[y + 1] = row(y) + time_step * tendency_row(row(y - 1), row(y), row(y + 1))

    @pl.loop(1, tall - 1, unroll=7)
    def _(y):
        first[y + 1] = base[y] + time_step * tendency_row(base[y - 1], base[y], base[y + 1])

    @pl.when(inside_down)
    def _():
        up_copy.wait_recv()

    @pl.when(jnp.logical_not(inside_down))
    def _():
        before[...] = jnp.zeros_like(before)

    @pl.when(inside_up)
    def _():
        down_copy.wait_recv()

    @pl.when(jnp.logical_not(inside_up))
    def _():
        after[...] = jnp.zeros_like(after)

    for y in (-1, 0, tall - 1, tall):
        section(y)
    first[0] = first[0] * jnp.where(inside_down, 1.0, 0.0)
    first[tall + 1] = first[tall + 1] * jnp.where(inside_up, 1.0, 0.0)

    for item in token_copies:
        item.wait_send()
    strip_peer.wait_send()
    state_copy.wait_send()

    @pl.when(inner)
    def _():
        strip_mate.wait_send()
        for item in field_copies:
            item.wait_send()

    @pl.when(inside_up)
    def _():
        up_copy.wait_send()

    @pl.when(inside_down)
    def _():
        down_copy.wait_send()


def second_kernel(base, first, out_ref):
    wide = base.shape[2] // 2
    lon = lax.axis_index("lon")
    here = pl.ds(pl.multiple_of(lon * wide, 128), wide)
    there = pl.ds(pl.multiple_of((1 - lon) * wide, 128), wide)
    rows = []
    for y in range(out_ref.shape[1]):
        y = y + pl.program_id(0) * out_ref.shape[1]
        second = tendency_row(first[y], first[y + 1], first[y + 2])
        rows.append(0.5 * (base[y] + first[y + 1] + time_step * second))
    value = jnp.swapaxes(jnp.stack(rows), 0, 1)
    out_ref[:, :, here] = value[:, :, 0:wide]
    out_ref[:, :, there] = value[:, :, wide:]


def body(sizes, tokens, ln_gain, w_query, w_keyval, w_out, w_dec, nudge, state):
    cols, width = tokens.shape[1:]
    channels = nudge.shape[0]
    length = state.shape[2] * sizes["lon"]
    tall = state.shape[1] // sizes["lon"]
    windows = cols // WIN
    patches = w_dec.shape[1]
    strip = 16
    chunks = chunk_bounds(windows)
    most = max(w1 - w0 for w0, w1 in chunks)
    count = len(chunks)
    cells = 2 * HALF * WIN
    hbm, vmem = pl.BlockSpec(memory_space=pl.ANY), pl.BlockSpec(memory_space=pltpu.VMEM)
    V = pltpu.VMEM
    edge_rows = V((2, channels, length), BF16)
    pieces = V((count, patches, most * HALF * WIN), BF16)
    scratch = [
        V((width, 3 * width), BF16), V((width, width), BF16), V(w_dec.shape, BF16), V((patches, width), BF16),
        V((length, length), BF16), V((length, length), BF16),
        V((HALF, cols, width), BF16), V((HALF, cols, width), BF16), V((HALF, strip, width), BF16),
        V((HALF * HALF, width), BF16), V((HALF * HALF, width), BF16),
        V((HALF * HALF, width), BF16), V((HALF * HALF, width), BF16),
        V((windows, cells, width), F32), V((windows, HALF * WIN, width), F32),
        V((windows, cells, 3 * width), BF16), V((windows, cells, width), BF16), V((most * cells, width), BF16),
        V((cells, 2 * width // HEADS), F32),
        V((channels, tall, length), F32),
        pieces, pieces, V((HALF * PATCH * channels, length), BF16),
        edge_rows, edge_rows, edge_rows, edge_rows,
        V((channels, 1), F32),
        pltpu.SemaphoreType.DMA((9,)), pltpu.SemaphoreType.DMA((2 * count + 5,)),
        pltpu.SemaphoreType.DMA((2 * count + 5,)),
    ]
    plain, patch, undo = filter_tables(length, KEEP, windows)
    nudged, first = pl.pallas_call(
        functools.partial(cycle_kernel, sizes["lat"], undo),
        out_shape=[
            pltpu.VMEM((tall, channels, length), F32),
            pltpu.VMEM((tall + 2, channels, length), F32),
        ],
        in_specs=[hbm] * 8 + [vmem] * 2,
        out_specs=[vmem, vmem],
        scratch_shapes=scratch,
        compiler_params=pltpu.CompilerParams(
            collective_id=0, has_side_effects=True, vmem_limit_bytes=56 * 2**20
        ),
        name="cycle",
    )(tokens, state, w_query, w_keyval, w_out, w_dec, jnp.asarray(plain), jnp.asarray(patch), ln_gain[None], nudge[None])
    return pl.pallas_call(
        second_kernel,
        out_shape=jax.ShapeDtypeStruct((channels, tall, length), F32),
        grid=(tall // 8,),
        in_specs=[vmem, vmem],
        out_specs=pl.BlockSpec((channels, 8, length), lambda g: (0, g, 0)),
        compiler_params=pltpu.CompilerParams(vmem_limit_bytes=16 * 2**20),
        name="second",
    )(nudged, first)


def solution(mesh):
    in_specs = (
        P(("member", "lat"), "lon", None),
        P(),
        P(),
        P(),
        P(),
        P(),
        P(),
        P(None, ("member", "lat"), "lon"),
    )
    out_specs = P(None, ("member", "lat", "lon"), None)
    return jax.shard_map(
        functools.partial(body, dict(mesh.shape)),
        mesh=mesh,
        in_specs=in_specs,
        out_specs=out_specs,
        check_vma=False,
    )
```

```python
import functools
import math

import jax
import jax.numpy as jnp
import ml_dtypes
import numpy as np
from jax import lax
from jax.experimental import pallas as pl
from jax.experimental.pallas import tpu as pltpu
from jax.sharding import PartitionSpec as P

HEADS = 16
WIN = 8
PATCH = 4
VARS = 4
LEV = 8
KEEP = 256

time_step = 0.1
diffusion = 0.5
epsilon = 1e-05
F32 = jnp.float32
BF16 = jnp.bfloat16
NT = (((1,), (1,)), ((), ()))
HALF = WIN // 2
MESH = pl.DeviceIdType.MESH


def chunk_bounds(windows):
    size = 4
    return [(w, min(w + size, windows)) for w in range(0, windows, size)]


def filter_tables(length, kept, windows):
    offset = np.arange(length)
    waves = np.arange(1, kept)
    angles = 2.0 * np.pi * ((offset[:, None] * waves[None, :]) % length) / length
    kernel = (1.0 + 2.0 * np.cos(angles).sum(1)) / length
    pixel = []
    for side in range(2):
        for w0, w1 in chunk_bounds(windows):
            for b in range(PATCH):
                column = np.arange(w0 * WIN, w1 * WIN) + HALF
                pixel.append(side * (length // 2) + PATCH * column + b)
    pixel = np.concatenate(pixel)
    plain = (offset[None, :] - offset[:, None]) % length
    patch = (offset[None, :] - pixel[:, None]) % length

    def rounded(factor):
        return (kernel * factor).astype(np.float32).astype(ml_dtypes.bfloat16)

    factors = 1.0 + np.arange(2048) / 2048
    errors = [np.square(rounded(f).astype(np.float64) / f - kernel).sum() for f in factors]
    factor = float(factors[int(np.argmin(errors))])
    return rounded(factor)[plain], rounded(factor)[patch], 1.0 / factor


def tendency_row(south, centre, north):
    channels, length = centre.shape
    west = pltpu.roll(centre, 1, 1)
    east = pltpu.roll(centre, length - 1, 1)
    u = centre[:LEV][None]
    v = centre[LEV : 2 * LEV][None]
    dx = (east - west).reshape(VARS, LEV, length)
    dy = (north - south).reshape(VARS, LEV, length)
    advection = ((u * dx + v * dy) * 0.5).reshape(channels, length)
    return diffusion * (east + west + north + south - 4.0 * centre) - advection


def cycle_kernel(
    n_lat, undo, tokens, state, wq_hbm, wkv_hbm, wo_hbm, wd_hbm, plain_hbm, patch_hbm, gain_ref, nudge_ref, base, first,
    wqkv, wo, wd, wdt, plain, patch, own, halo, side, strip_own, strip_far, edge_own, edge_halo,
    xs, normed, qkv, att, lo, bias, band, sent, came, held, up_rows, down_rows, before, after, strength,
    load_sem, send_sem, recv_sem,
):
    lat, lon = lax.axis_index("lat"), lax.axis_index("lon")
    peer = 1 - lon
    cols, width = tokens.shape[1:]
    windows = cols // WIN
    cells = 2 * HALF * WIN
    tall, channels, length = base.shape
    wide = length // 2
    chunks = chunk_bounds(windows)
    count = len(chunks)
    is_low = lon == 0
    has_prev, has_next = lat > 0, lat < n_lat - 1
    prev, nxt = jnp.maximum(lat - 1, 0), jnp.minimum(lat + 1, n_lat - 1)
    inner = jnp.where(is_low, has_prev, has_next)
    more = jnp.where(is_low, has_next, has_prev)
    ring = {"lat": jnp.where(is_low, nxt, prev), "lon": jnp.where(more, lon, peer)}
    mate = {"lat": jnp.where(is_low, prev, nxt), "lon": peer}
    side_by = {"lat": lat, "lon": peer}

    def load(i, src, dst):
        return pltpu.make_async_copy(src, dst, load_sem.at[i])

    def remote(i, src, dst, to):
        return pltpu.make_async_remote_copy(
            src_ref=src, dst_ref=dst, send_sem=send_sem.at[i], recv_sem=recv_sem.at[i],
            device_id=to, device_id_type=MESH,
        )

    own_at = pl.multiple_of(lon * HALF, HALF)
    far_at = pl.multiple_of(peer * HALF, HALF)
    strip = side.shape[1]
    side_load = load(0, tokens.at[pl.ds(far_at, HALF), pl.ds(0, strip), :], side)
    own_load = load(1, tokens.at[pl.ds(own_at, HALF)], own)
    dec_load = load(2, wd_hbm, wd)
    query_load = load(3, wq_hbm, wqkv.at[:, pl.ds(0, width)])
    keyval_load = load(4, wkv_hbm, wqkv.at[:, pl.ds(width, 2 * width)])
    my_rows = pl.ds(pl.multiple_of(lon * tall, 8), tall)
    peer_rows = pl.ds(pl.multiple_of(peer * tall, 8), tall)
    state_load = load(5, state.at[:, my_rows, :], band.at[:, :, pl.ds(0, wide)])
    plain_load = load(6, plain_hbm, plain)
    out_load = load(7, wo_hbm, wo)
    patch_load = load(8, patch_hbm, patch)
    side_load.start()
    own_load.start()

    barrier = pltpu.get_barrier_semaphore()

    def greet(to):
        pl.semaphore_signal(barrier, inc=1, device_id=to, device_id_type=MESH)

    greet(side_by)

    @pl.when(has_prev)
    def _():
        greet({"lat": prev, "lon": lon})

    @pl.when(has_next)
    def _():
        greet({"lat": nxt, "lon": lon})

    @pl.when(inner)
    def _():
        greet(mate)

    pl.semaphore_wait(
        barrier, 1 + has_prev.astype(jnp.int32) + has_next.astype(jnp.int32) + inner.astype(jnp.int32)
    )

    ends = [min(cols, -(-(w1 * WIN + HALF) // strip) * strip) for _, w1 in chunks]
    token_copies = []
    for i, (begin, end) in enumerate(zip([0] + ends[:-1], ends)):
        at = pl.ds(begin, end - begin)
        token_copies.append(remote(i, tokens.at[pl.ds(far_at, HALF), at, :], halo.at[:, at, :], ring))
    token_copies[0].start()
    for item in (dec_load, query_load, keyval_load, state_load, plain_load, out_load, patch_load):
        item.start()
    base_id = count
    state_copy = remote(base_id, state.at[:, peer_rows, :], band.at[:, :, pl.ds(wide, wide)], side_by)
    strip_peer = remote(base_id + 1, strip_far, edge_own, side_by)
    strip_mate = remote(base_id + 2, strip_own, edge_halo, mate)
    field_copies = [remote(base_id + 3 + i, sent.at[i], came.at[i], mate) for i in range(count)]
    up_copy_id, down_copy_id = base_id + 3 + count, base_id + 4 + count

    def pack(source, out):
        for r in range(0, HALF, 2):
            pair = [source[r + j, 0:WIN, :].astype(F32)[:HALF] for j in range(2)]
            out[r * HALF : (r + 2) * HALF, :] = jnp.concatenate(pair, axis=0).astype(BF16)

    side_load.wait()
    pack(side, strip_far)
    strip_peer.start()
    own_load.wait()
    pack(own, strip_own)

    @pl.when(inner)
    def _():
        strip_mate.start()

    @pl.when(jnp.logical_not(inner))
    def _():
        edge_halo[...] = strip_own[...]

    state_copy.start()

    def normalize(source, edge, w0, w1, at):
        c0, c1 = w0 * WIN, w1 * WIN
        n = w1 - w0
        for r in range(HALF):
            if c1 < cols:
                block = source[r, c0 : c1 + WIN, :].astype(F32)[HALF : HALF + n * WIN]
            else:
                block = source[r, c0:c1, :].astype(F32)[HALF:]
                r0 = r // 2 * WIN
                tail = edge[r0 : r0 + WIN, :].astype(F32)[r % 2 * HALF : r % 2 * HALF + HALF]
                block = jnp.concatenate([block, tail], axis=0)
            centred = block - jnp.mean(block, axis=-1, keepdims=True)
            variance = jnp.mean(centred * centred, axis=-1, keepdims=True)
            unit = centred * lax.rsqrt(variance + epsilon) * gain_ref[...]
            xs[w0:w1, at + r * WIN : at + (r + 1) * WIN, :] = block.reshape(n, WIN, width)
            normed[w0:w1, r * WIN : (r + 1) * WIN, :] = unit.reshape(n, WIN, width)

    scale = math.log2(math.e) / math.sqrt(width // HEADS)

    def project(w0, w1, at):
        n = w1 - w0
        flat = normed[w0:w1].reshape(n * HALF * WIN, width).astype(BF16)
        for part in range(3):
            on = slice(part * width, (part + 1) * width)
            value = jnp.dot(flat, wqkv[:, on], preferred_element_type=F32)
            if part == 0:
                value = value * scale
            qkv[w0:w1, at : at + HALF * WIN, on] = value.astype(BF16).reshape(n, HALF * WIN, width)

    def attend(w0, w1):
        head = width // HEADS
        pair = 2 * head
        lanes = lax.broadcasted_iota(jnp.int32, (cells, pair), 1) < head
        left = lax.broadcasted_iota(jnp.int32, (2 * cells, pair), 1) < head
        upper = lax.broadcasted_iota(jnp.int32, (2 * cells, pair), 0) < cells
        ones = (left == upper).astype(F32).astype(BF16)

        def both(x):
            zero = jnp.zeros_like(x)
            return jnp.concatenate([jnp.where(lanes, x, zero), jnp.where(lanes, zero, x)], axis=0)

        @pl.loop(w0, w1, unroll=w1 - w0)
        def _(w):
            spots = [p * pair for p in range(HEADS // 2)]
            scores = []
            for on in spots:
                q = qkv[w, :, on : on + pair]
                k = both(qkv[w, :, width + on : width + on + pair])
                scores.append(lax.dot_general(q, k, NT, preferred_element_type=F32) + bias[...])
            powers = []
            for s in scores:
                low = jnp.max(jnp.where(lanes, s, -jnp.inf), axis=-1, keepdims=True)
                high = jnp.max(jnp.where(lanes, -jnp.inf, s), axis=-1, keepdims=True)
                powers.append(jnp.exp2(s - jnp.where(lanes, low, high)).astype(BF16))
            mixed = []
            for on, e in zip(spots, powers):
                v = both(qkv[w, :, 2 * width + on : 2 * width + on + pair])
                o = jnp.dot(e, jnp.concatenate([v, ones], axis=1), preferred_element_type=F32)
                mixed.append((o[:, :pair] / o[:, pair:]).astype(BF16))
            att[w] = jnp.concatenate(mixed, axis=1)

    patches = wdt.shape[0]
    part = PATCH * channels

    def place(value, at, n):
        for r in range(HALF):
            pieces = [value[b * part : (b + 1) * part, r * n : (r + 1) * n] for b in range(PATCH)]
            held[r * part : (r + 1) * part, at : at + PATCH * n] = jnp.concatenate(pieces, axis=1)

    def decode(i):
        w0, w1 = chunks[i]
        n = w1 - w0
        mixed = att[w0:w1].reshape(n * cells, width)
        for at in range(0, width, 512):
            update = jnp.dot(mixed, wo[:, at : at + 512], preferred_element_type=F32)
            value = xs[w0:w1, :, at : at + 512] + update.reshape(n, cells, 512)
            value = value.reshape(n, 2 * HALF, WIN, 512)
            value = jnp.swapaxes(value, 0, 1).reshape(n * cells, 512)
            lo[0 : n * cells, at : at + 512] = value.astype(BF16)
        value = lax.dot_general(wdt[...], lo[0 : n * cells, :], NT, preferred_element_type=F32).astype(BF16)
        here = n * HALF * WIN
        sent[i] = value[:, here:]

        @pl.when(inner)
        def _():
            field_copies[i].start()

        @pl.when(jnp.logical_not(inner))
        def _():
            came[i] = sent[i]

        place(value[:, :here], w0 * WIN * PATCH, n * WIN)

    dec_load.wait()
    row_id = lax.broadcasted_iota(jnp.int32, (patches, patches), 0)
    col_id = lax.broadcasted_iota(jnp.int32, (patches, patches), 1)
    area = PATCH * PATCH
    wanted = (row_id % channels) * area + (row_id // channels) % PATCH * PATCH + row_id // part
    chosen = (col_id == wanted).astype(F32).astype(BF16)
    wdt[...] = lax.dot_general(chosen, wd[...], NT, preferred_element_type=F32).astype(BF16)

    q_id = lax.broadcasted_iota(jnp.int32, bias.shape, 0) // (HALF * WIN)
    k_id = lax.broadcasted_iota(jnp.int32, bias.shape, 1) // (HALF * WIN) % 2
    bias[...] = jnp.where((q_id != k_id) & jnp.logical_not(inner), -1e30, 0.0).astype(F32)
    eye = lax.broadcasted_iota(jnp.int32, (channels, channels), 0)
    eye = eye == lax.broadcasted_iota(jnp.int32, (channels, channels), 1)
    strength[...] = jnp.sum(jnp.where(eye, nudge_ref[...], 0.0), axis=1, keepdims=True) * undo

    strip_peer.wait_recv()
    normalize(own, edge_own, 0, windows, 0)
    query_load.wait()
    keyval_load.wait()
    project(0, windows, 0)

    state_load.wait()
    state_copy.wait_recv()
    plain_load.wait()

    @pl.loop(0, channels // LEV)
    def _(g):
        on = pl.ds(pl.multiple_of(g * LEV, LEV), LEV)
        s = band[on].reshape(LEV * tall, length)
        kept = jnp.dot(s.astype(BF16), plain[...], preferred_element_type=F32)
        kept = s.reshape(LEV, tall, length) - strength[on][:, :, None] * kept.reshape(LEV, tall, length)
        base[:, on, :] = jnp.swapaxes(kept, 0, 1)

    out_load.wait()

    @pl.when(inner)
    def _():
        strip_mate.wait_recv()

    token_copies[0].wait_recv()
    token_copies[1].start()
    for i, (w0, w1) in enumerate(chunks):
        normalize(halo, edge_halo, w0, w1, HALF * WIN)
        project(w0, w1, HALF * WIN)
        attend(w0, w1)
        if i < count - 1:
            if i + 2 < count:
                token_copies[i + 2].start()
            token_copies[i + 1].wait_recv()
        decode(i)

    patch_load.wait()
    for i, (w0, w1) in enumerate(chunks):
        n = (w1 - w0) * WIN
        last = i == count - 1
        at = wide + w0 * WIN * PATCH
        if last:
            for lane in range(0, length, 256):
                kept = jnp.dot(held[:, 0:at], patch[0:at, lane : lane + 256], preferred_element_type=F32)
                kept = strength[...][None] * kept.reshape(tall, channels, 256)
                base[:, :, lane : lane + 256] = base[:, :, lane : lane + 256] + kept

        @pl.when(inner)
        def _():
            field_copies[i].wait_recv()

        place(came[i], at, n)

    last_at = wide + chunks[-1][0] * WIN * PATCH

    def nudge_rows(r, n):
        at, y = pl.multiple_of(r * part, part), r * PATCH
        kept = jnp.dot(held[pl.ds(at, n * part), last_at:], patch[last_at:, :], preferred_element_type=F32)
        rows = pl.ds(y, n * PATCH)
        base[rows] = base[rows] + strength[...][None] * kept.reshape(n * PATCH, channels, length)

    def turned(value):
        return jnp.concatenate([value[..., wide:], value[..., :wide]], axis=-1).astype(BF16)

    up_to = {"lat": jnp.where(is_low, lat, nxt), "lon": peer}
    down_to = {"lat": jnp.where(is_low, prev, lat), "lon": peer}
    inside_up, inside_down = is_low | has_next, jnp.logical_not(is_low) | has_prev
    up_copy = remote(up_copy_id, up_rows, before, up_to)
    down_copy = remote(down_copy_id, down_rows, after, down_to)

    def send_up():
        up_rows[...] = turned(base[tall - 2 : tall])
        up_copy.start()

    def send_down():
        down_rows[...] = turned(base[0:2])
        down_copy.start()

    nudge_rows(jnp.where(is_low, 0, HALF - 1), 1)
    pl.when(is_low & has_prev)(send_down)
    pl.when(jnp.logical_not(is_low) & has_next)(send_up)
    nudge_rows(jnp.where(is_low, HALF - 1, 0), 1)
    pl.when(is_low)(send_up)
    pl.when(jnp.logical_not(is_low))(send_down)
    nudge_rows(1, HALF - 2)

    def row(y):
        if y < 0:
            return before[y + 2].astype(F32)
        if y >= tall:
            return after[y - tall].astype(F32)
        return base[y]

    def section(y):
        first[y + 1] = row(y) + time_step * tendency_row(row(y - 1), row(y), row(y + 1))

    @pl.loop(1, tall - 1, unroll=7)
    def _(y):
        first[y + 1] = base[y] + time_step * tendency_row(base[y - 1], base[y], base[y + 1])

    @pl.loop(2, tall - 2, unroll=4)
    def _(y):
        second = tendency_row(first[y], first[y + 1], first[y + 2])
        base[y] = 0.5 * (base[y] + first[y + 1] + time_step * second)

    @pl.when(inside_down)
    def _():
        up_copy.wait_recv()

    @pl.when(jnp.logical_not(inside_down))
    def _():
        before[...] = jnp.zeros_like(before)

    @pl.when(inside_up)
    def _():
        down_copy.wait_recv()

    @pl.when(jnp.logical_not(inside_up))
    def _():
        after[...] = jnp.zeros_like(after)

    for y in (-1, 0, tall - 1, tall):
        section(y)
    first[0] = first[0] * jnp.where(inside_down, 1.0, 0.0)
    first[tall + 1] = first[tall + 1] * jnp.where(inside_up, 1.0, 0.0)

    for item in token_copies:
        item.wait_send()
    strip_peer.wait_send()
    state_copy.wait_send()

    @pl.when(inner)
    def _():
        strip_mate.wait_send()
        for item in field_copies:
            item.wait_send()

    @pl.when(inside_up)
    def _():
        up_copy.wait_send()

    @pl.when(inside_down)
    def _():
        down_copy.wait_send()


def second_kernel(base, first, out_ref):
    wide = base.shape[2] // 2
    lon = lax.axis_index("lon")
    here = pl.ds(pl.multiple_of(lon * wide, 128), wide)
    there = pl.ds(pl.multiple_of((1 - lon) * wide, 128), wide)
    rows = []
    tall, block = base.shape[0], out_ref.shape[1]
    for k in range(block):
        y = k + pl.program_id(0) * block
        row = base[y]
        if k < 2 or k >= block - 2:
            second = tendency_row(first[y], first[y + 1], first[y + 2])
            done = 0.5 * (row + first[y + 1] + time_step * second)
            row = jnp.where((y < 2) | (y >= tall - 2), done, row)
        rows.append(row)
    value = jnp.swapaxes(jnp.stack(rows), 0, 1)
    out_ref[:, :, here] = value[:, :, 0:wide]
    out_ref[:, :, there] = value[:, :, wide:]


def body(sizes, tokens, ln_gain, w_query, w_keyval, w_out, w_dec, nudge, state):
    cols, width = tokens.shape[1:]
    channels = nudge.shape[0]
    length = state.shape[2] * sizes["lon"]
    tall = state.shape[1] // sizes["lon"]
    windows = cols // WIN
    patches = w_dec.shape[1]
    strip = 16
    chunks = chunk_bounds(windows)
    most = max(w1 - w0 for w0, w1 in chunks)
    count = len(chunks)
    cells = 2 * HALF * WIN
    hbm, vmem = pl.BlockSpec(memory_space=pl.ANY), pl.BlockSpec(memory_space=pltpu.VMEM)
    V = pltpu.VMEM
    edge_rows = V((2, channels, length), BF16)
    pieces = V((count, patches, most * HALF * WIN), BF16)
    scratch = [
        V((width, 3 * width), BF16), V((width, width), BF16), V(w_dec.shape, BF16), V((patches, width), BF16),
        V((length, length), BF16), V((length, length), BF16),
        V((HALF, cols, width), BF16), V((HALF, cols, width), BF16), V((HALF, strip, width), BF16),
        V((HALF * HALF, width), BF16), V((HALF * HALF, width), BF16),
        V((HALF * HALF, width), BF16), V((HALF * HALF, width), BF16),
        V((windows, cells, width), F32), V((windows, HALF * WIN, width), F32),
        V((windows, cells, 3 * width), BF16), V((windows, cells, width), BF16), V((most * cells, width), BF16),
        V((cells, 2 * width // HEADS), F32),
        V((channels, tall, length), F32),
        pieces, pieces, V((HALF * PATCH * channels, length), BF16),
        edge_rows, edge_rows, edge_rows, edge_rows,
        V((channels, 1), F32),
        pltpu.SemaphoreType.DMA((9,)), pltpu.SemaphoreType.DMA((2 * count + 5,)),
        pltpu.SemaphoreType.DMA((2 * count + 5,)),
    ]
    plain, patch, undo = filter_tables(length, KEEP, windows)
    nudged, first = pl.pallas_call(
        functools.partial(cycle_kernel, sizes["lat"], undo),
        out_shape=[
            pltpu.VMEM((tall, channels, length), F32),
            pltpu.VMEM((tall + 2, channels, length), F32),
        ],
        in_specs=[hbm] * 8 + [vmem] * 2,
        out_specs=[vmem, vmem],
        scratch_shapes=scratch,
        compiler_params=pltpu.CompilerParams(
            collective_id=0, has_side_effects=True, vmem_limit_bytes=56 * 2**20
        ),
        name="cycle",
    )(tokens, state, w_query, w_keyval, w_out, w_dec, jnp.asarray(plain), jnp.asarray(patch), ln_gain[None], nudge[None])
    return pl.pallas_call(
        second_kernel,
        out_shape=jax.ShapeDtypeStruct((channels, tall, length), F32),
        grid=(tall // 8,),
        in_specs=[vmem, vmem],
        out_specs=pl.BlockSpec((channels, 8, length), lambda g: (0, g, 0)),
        compiler_params=pltpu.CompilerParams(vmem_limit_bytes=16 * 2**20),
        name="second",
    )(nudged, first)


def solution(mesh):
    in_specs = (
        P(("member", "lat"), "lon", None),
        P(),
        P(),
        P(),
        P(),
        P(),
        P(),
        P(None, ("member", "lat"), "lon"),
    )
    out_specs = P(None, ("member", "lat", "lon"), None)
    return jax.shard_map(
        functools.partial(body, dict(mesh.shape)),
        mesh=mesh,
        in_specs=in_specs,
        out_specs=out_specs,
        check_vma=False,
    )
```

```python
import functools
import math

import jax
import jax.numpy as jnp
import ml_dtypes
import numpy as np
from jax import lax
from jax.experimental import pallas as pl
from jax.experimental.pallas import tpu as pltpu
from jax.sharding import PartitionSpec as P

HEADS = 16
WIN = 8
PATCH = 4
VARS = 4
LEV = 8
KEEP = 256

time_step = 0.1
diffusion = 0.5
epsilon = 1e-05
F32 = jnp.float32
BF16 = jnp.bfloat16
NT = (((1,), (1,)), ((), ()))
HALF = WIN // 2
MESH = pl.DeviceIdType.MESH


def chunk_bounds(windows):
    size = 4
    return [(w, min(w + size, windows)) for w in range(0, windows, size)]


def filter_tables(length, kept, windows):
    offset = np.arange(length)
    waves = np.arange(1, kept)
    angles = 2.0 * np.pi * ((offset[:, None] * waves[None, :]) % length) / length
    kernel = (1.0 + 2.0 * np.cos(angles).sum(1)) / length
    pixel = []
    for side in range(2):
        for w0, w1 in chunk_bounds(windows):
            for b in range(PATCH):
                column = np.arange(w0 * WIN, w1 * WIN) + HALF
                pixel.append(side * (length // 2) + PATCH * column + b)
    pixel = np.concatenate(pixel)
    plain = (offset[None, :] - offset[:, None]) % length
    patch = (offset[None, :] - pixel[:, None]) % length

    def rounded(factor):
        return (kernel * factor).astype(np.float32).astype(ml_dtypes.bfloat16)

    factors = 1.0 + np.arange(2048) / 2048
    errors = [np.square(rounded(f).astype(np.float64) / f - kernel).sum() for f in factors]
    factor = float(factors[int(np.argmin(errors))])
    return rounded(factor)[plain], rounded(factor)[patch], 1.0 / factor


def tendency_row(south, centre, north):
    channels, length = centre.shape
    west = pltpu.roll(centre, 1, 1)
    east = pltpu.roll(centre, length - 1, 1)
    u = centre[:LEV][None]
    v = centre[LEV : 2 * LEV][None]
    dx = (east - west).reshape(VARS, LEV, length)
    dy = (north - south).reshape(VARS, LEV, length)
    advection = ((u * dx + v * dy) * 0.5).reshape(channels, length)
    return diffusion * (east + west + north + south - 4.0 * centre) - advection


def cycle_kernel(
    n_lat, undo, tokens, state, wq_hbm, wkv_hbm, wo_hbm, wd_hbm, plain_hbm, patch_hbm, gain_ref, nudge_ref, base, first,
    wqkv, wo, wd, wdt, plain, patch, own, halo, side, strip_own, strip_far, edge_own, edge_halo,
    xs, normed, qkv, att, lo, bias, band, sent, came, held, up_rows, down_rows, before, after, strength,
    load_sem, send_sem, recv_sem,
):
    lat, lon = lax.axis_index("lat"), lax.axis_index("lon")
    peer = 1 - lon
    cols, width = tokens.shape[1:]
    windows = cols // WIN
    cells = 2 * HALF * WIN
    tall, channels, length = base.shape
    wide = length // 2
    chunks = chunk_bounds(windows)
    count = len(chunks)
    is_low = lon == 0
    has_prev, has_next = lat > 0, lat < n_lat - 1
    prev, nxt = jnp.maximum(lat - 1, 0), jnp.minimum(lat + 1, n_lat - 1)
    inner = jnp.where(is_low, has_prev, has_next)
    more = jnp.where(is_low, has_next, has_prev)
    ring = {"lat": jnp.where(is_low, nxt, prev), "lon": jnp.where(more, lon, peer)}
    mate = {"lat": jnp.where(is_low, prev, nxt), "lon": peer}
    side_by = {"lat": lat, "lon": peer}

    def load(i, src, dst):
        return pltpu.make_async_copy(src, dst, load_sem.at[i])

    def remote(i, src, dst, to):
        return pltpu.make_async_remote_copy(
            src_ref=src, dst_ref=dst, send_sem=send_sem.at[i], recv_sem=recv_sem.at[i],
            device_id=to, device_id_type=MESH,
        )

    own_at = pl.multiple_of(lon * HALF, HALF)
    far_at = pl.multiple_of(peer * HALF, HALF)
    strip = side.shape[1]
    side_load = load(0, tokens.at[pl.ds(far_at, HALF), pl.ds(0, strip), :], side)
    own_load = load(1, tokens.at[pl.ds(own_at, HALF)], own)
    dec_load = load(2, wd_hbm, wd)
    query_load = load(3, wq_hbm, wqkv.at[:, pl.ds(0, width)])
    keyval_load = load(4, wkv_hbm, wqkv.at[:, pl.ds(width, 2 * width)])
    my_rows = pl.ds(pl.multiple_of(lon * tall, 8), tall)
    peer_rows = pl.ds(pl.multiple_of(peer * tall, 8), tall)
    state_load = load(5, state.at[:, my_rows, :], band.at[:, :, pl.ds(0, wide)])
    plain_load = load(6, plain_hbm, plain)
    out_load = load(7, wo_hbm, wo)
    patch_load = load(8, patch_hbm, patch)
    side_load.start()
    own_load.start()

    barrier = pltpu.get_barrier_semaphore()

    def greet(to):
        pl.semaphore_signal(barrier, inc=1, device_id=to, device_id_type=MESH)

    greet(side_by)

    @pl.when(has_prev)
    def _():
        greet({"lat": prev, "lon": lon})

    @pl.when(has_next)
    def _():
        greet({"lat": nxt, "lon": lon})

    @pl.when(inner)
    def _():
        greet(mate)

    pl.semaphore_wait(
        barrier, 1 + has_prev.astype(jnp.int32) + has_next.astype(jnp.int32) + inner.astype(jnp.int32)
    )

    ends = [min(cols, -(-(w1 * WIN + HALF) // strip) * strip) for _, w1 in chunks]
    token_copies = []
    for i, (begin, end) in enumerate(zip([0] + ends[:-1], ends)):
        at = pl.ds(begin, end - begin)
        token_copies.append(remote(i, tokens.at[pl.ds(far_at, HALF), at, :], halo.at[:, at, :], ring))
    token_copies[0].start()
    for item in (dec_load, query_load, keyval_load, state_load, plain_load, out_load, patch_load):
        item.start()
    base_id = count
    state_copy = remote(base_id, state.at[:, peer_rows, :], band.at[:, :, pl.ds(wide, wide)], side_by)
    strip_peer = remote(base_id + 1, strip_far, edge_own, side_by)
    strip_mate = remote(base_id + 2, strip_own, edge_halo, mate)
    field_copies = [remote(base_id + 3 + i, sent.at[i], came.at[i], mate) for i in range(count)]
    up_copy_id, down_copy_id = base_id + 3 + count, base_id + 4 + count

    def pack(source, out):
        for r in range(0, HALF, 2):
            pair = [source[r + j, 0:WIN, :].astype(F32)[:HALF] for j in range(2)]
            out[r * HALF : (r + 2) * HALF, :] = jnp.concatenate(pair, axis=0).astype(BF16)

    side_load.wait()
    pack(side, strip_far)
    strip_peer.start()
    own_load.wait()
    pack(own, strip_own)

    @pl.when(inner)
    def _():
        strip_mate.start()

    @pl.when(jnp.logical_not(inner))
    def _():
        edge_halo[...] = strip_own[...]

    state_copy.start()

    def normalize(source, edge, w0, w1, at):
        c0, c1 = w0 * WIN, w1 * WIN
        n = w1 - w0
        for r in range(HALF):
            if c1 < cols:
                block = source[r, c0 : c1 + WIN, :].astype(F32)[HALF : HALF + n * WIN]
            else:
                block = source[r, c0:c1, :].astype(F32)[HALF:]
                r0 = r // 2 * WIN
                tail = edge[r0 : r0 + WIN, :].astype(F32)[r % 2 * HALF : r % 2 * HALF + HALF]
                block = jnp.concatenate([block, tail], axis=0)
            centred = block - jnp.mean(block, axis=-1, keepdims=True)
            variance = jnp.mean(centred * centred, axis=-1, keepdims=True)
            unit = centred * lax.rsqrt(variance + epsilon) * gain_ref[...]
            xs[w0:w1, at + r * WIN : at + (r + 1) * WIN, :] = block.reshape(n, WIN, width)
            normed[w0:w1, r * WIN : (r + 1) * WIN, :] = unit.reshape(n, WIN, width)

    scale = math.log2(math.e) / math.sqrt(width // HEADS)

    def project(w0, w1, at):
        n = w1 - w0
        flat = normed[w0:w1].reshape(n * HALF * WIN, width).astype(BF16)
        for part in range(3):
            on = slice(part * width, (part + 1) * width)
            value = jnp.dot(flat, wqkv[:, on], preferred_element_type=F32)
            if part == 0:
                value = value * scale
            qkv[w0:w1, at : at + HALF * WIN, on] = value.astype(BF16).reshape(n, HALF * WIN, width)

    def attend(w0, w1):
        head = width // HEADS
        pair = 2 * head
        lanes = lax.broadcasted_iota(jnp.int32, (cells, pair), 1) < head
        left = lax.broadcasted_iota(jnp.int32, (2 * cells, pair), 1) < head
        upper = lax.broadcasted_iota(jnp.int32, (2 * cells, pair), 0) < cells
        ones = (left == upper).astype(F32).astype(BF16)

        def both(x):
            zero = jnp.zeros_like(x)
            return jnp.concatenate([jnp.where(lanes, x, zero), jnp.where(lanes, zero, x)], axis=0)

        @pl.loop(w0, w1, unroll=w1 - w0)
        def _(w):
            spots = [p * pair for p in range(HEADS // 2)]
            scores = []
            for on in spots:
                q = qkv[w, :, on : on + pair]
                k = both(qkv[w, :, width + on : width + on + pair])
                scores.append(lax.dot_general(q, k, NT, preferred_element_type=F32) + bias[...])
            powers = []
            for s in scores:
                low = jnp.max(jnp.where(lanes, s, -jnp.inf), axis=-1, keepdims=True)
                high = jnp.max(jnp.where(lanes, -jnp.inf, s), axis=-1, keepdims=True)
                powers.append(jnp.exp2(s - jnp.where(lanes, low, high)).astype(BF16))
            mixed = []
            for on, e in zip(spots, powers):
                v = both(qkv[w, :, 2 * width + on : 2 * width + on + pair])
                o = jnp.dot(e, jnp.concatenate([v, ones], axis=1), preferred_element_type=F32)
                mixed.append((o[:, :pair] / o[:, pair:]).astype(BF16))
            att[w] = jnp.concatenate(mixed, axis=1)

    patches = wdt.shape[0]
    part = PATCH * channels

    def place(value, at, n):
        for r in range(HALF):
            pieces = [value[b * part : (b + 1) * part, r * n : (r + 1) * n] for b in range(PATCH)]
            held[r * part : (r + 1) * part, at : at + PATCH * n] = jnp.concatenate(pieces, axis=1)

    def decode(i):
        w0, w1 = chunks[i]
        n = w1 - w0
        mixed = att[w0:w1].reshape(n * cells, width)
        for at in range(0, width, 512):
            update = jnp.dot(mixed, wo[:, at : at + 512], preferred_element_type=F32)
            value = xs[w0:w1, :, at : at + 512] + update.reshape(n, cells, 512)
            value = value.reshape(n, 2 * HALF, WIN, 512)
            value = jnp.swapaxes(value, 0, 1).reshape(n * cells, 512)
            lo[0 : n * cells, at : at + 512] = value.astype(BF16)
        value = lax.dot_general(wdt[...], lo[0 : n * cells, :], NT, preferred_element_type=F32).astype(BF16)
        here = n * HALF * WIN
        sent[i] = value[:, here:]

        @pl.when(inner)
        def _():
            field_copies[i].start()

        @pl.when(jnp.logical_not(inner))
        def _():
            came[i] = sent[i]

        place(value[:, :here], w0 * WIN * PATCH, n * WIN)

    dec_load.wait()
    row_id = lax.broadcasted_iota(jnp.int32, (patches, patches), 0)
    col_id = lax.broadcasted_iota(jnp.int32, (patches, patches), 1)
    area = PATCH * PATCH
    wanted = (row_id % channels) * area + (row_id // channels) % PATCH * PATCH + row_id // part
    chosen = (col_id == wanted).astype(F32).astype(BF16)
    wdt[...] = lax.dot_general(chosen, wd[...], NT, preferred_element_type=F32).astype(BF16)

    q_id = lax.broadcasted_iota(jnp.int32, bias.shape, 0) // (HALF * WIN)
    k_id = lax.broadcasted_iota(jnp.int32, bias.shape, 1) // (HALF * WIN) % 2
    bias[...] = jnp.where((q_id != k_id) & jnp.logical_not(inner), -1e30, 0.0).astype(F32)
    eye = lax.broadcasted_iota(jnp.int32, (channels, channels), 0)
    eye = eye == lax.broadcasted_iota(jnp.int32, (channels, channels), 1)
    strength[...] = jnp.sum(jnp.where(eye, nudge_ref[...], 0.0), axis=1, keepdims=True) * undo

    strip_peer.wait_recv()
    normalize(own, edge_own, 0, windows, 0)
    query_load.wait()
    keyval_load.wait()
    project(0, windows, 0)

    state_load.wait()
    state_copy.wait_recv()
    plain_load.wait()

    @pl.loop(0, channels // LEV)
    def _(g):
        on = pl.ds(pl.multiple_of(g * LEV, LEV), LEV)
        s = band[on].reshape(LEV * tall, length)
        kept = jnp.dot(s.astype(BF16), plain[...], preferred_element_type=F32)
        kept = s.reshape(LEV, tall, length) - strength[on][:, :, None] * kept.reshape(LEV, tall, length)
        base[:, on, :] = jnp.swapaxes(kept, 0, 1)

    out_load.wait()

    @pl.when(inner)
    def _():
        strip_mate.wait_recv()

    token_copies[0].wait_recv()
    token_copies[1].start()
    for i, (w0, w1) in enumerate(chunks):
        normalize(halo, edge_halo, w0, w1, HALF * WIN)
        project(w0, w1, HALF * WIN)
        attend(w0, w1)
        if i < count - 1:
            if i + 2 < count:
                token_copies[i + 2].start()
            token_copies[i + 1].wait_recv()
        decode(i)

    patch_load.wait()
    for i, (w0, w1) in enumerate(chunks):
        n = (w1 - w0) * WIN
        last = i == count - 1
        at = wide + w0 * WIN * PATCH
        if last:
            for lane in range(0, length, 256):
                kept = jnp.dot(held[:, 0:at], patch[0:at, lane : lane + 256], preferred_element_type=F32)
                kept = strength[...][None] * kept.reshape(tall, channels, 256)
                base[:, :, lane : lane + 256] = base[:, :, lane : lane + 256] + kept

        @pl.when(inner)
        def _():
            field_copies[i].wait_recv()

        place(came[i], at, n)

    last_at = wide + chunks[-1][0] * WIN * PATCH

    def nudge_rows(r, n):
        at, y = pl.multiple_of(r * part, part), r * PATCH
        kept = jnp.dot(held[pl.ds(at, n * part), last_at:], patch[last_at:, :], preferred_element_type=F32)
        rows = pl.ds(y, n * PATCH)
        base[rows] = base[rows] + strength[...][None] * kept.reshape(n * PATCH, channels, length)

    def turned(value):
        return jnp.concatenate([value[..., wide:], value[..., :wide]], axis=-1).astype(BF16)

    up_to = {"lat": jnp.where(is_low, lat, nxt), "lon": peer}
    down_to = {"lat": jnp.where(is_low, prev, lat), "lon": peer}
    inside_up, inside_down = is_low | has_next, jnp.logical_not(is_low) | has_prev
    up_copy = remote(up_copy_id, up_rows, before, up_to)
    down_copy = remote(down_copy_id, down_rows, after, down_to)

    def send_up():
        up_rows[...] = turned(base[tall - 2 : tall])
        up_copy.start()

    def send_down():
        down_rows[...] = turned(base[0:2])
        down_copy.start()

    nudge_rows(jnp.where(is_low, 0, HALF - 1), 1)
    pl.when(is_low & has_prev)(send_down)
    pl.when(jnp.logical_not(is_low) & has_next)(send_up)
    nudge_rows(jnp.where(is_low, HALF - 1, 0), 1)
    pl.when(is_low)(send_up)
    pl.when(jnp.logical_not(is_low))(send_down)
    nudge_rows(1, HALF - 2)

    def row(y):
        if y < 0:
            return before[y + 2].astype(F32)
        if y >= tall:
            return after[y - tall].astype(F32)
        return base[y]

    def section(y):
        first[y + 1] = row(y) + time_step * tendency_row(row(y - 1), row(y), row(y + 1))

    @pl.loop(1, tall - 1, unroll=7)
    def _(y):
        first[y + 1] = base[y] + time_step * tendency_row(base[y - 1], base[y], base[y + 1])

    @pl.loop(2, tall - 2, unroll=4)
    def _(y):
        second = tendency_row(first[y], first[y + 1], first[y + 2])
        base[y] = 0.5 * (base[y] + first[y + 1] + time_step * second)

    def below():
        @pl.when(inside_down)
        def _():
            up_copy.wait_recv()

        @pl.when(jnp.logical_not(inside_down))
        def _():
            before[...] = jnp.zeros_like(before)

        section(-1)
        section(0)

    def above():
        @pl.when(inside_up)
        def _():
            down_copy.wait_recv()

        @pl.when(jnp.logical_not(inside_up))
        def _():
            after[...] = jnp.zeros_like(after)

        section(tall - 1)
        section(tall)

    pl.when(is_low)(above)
    below()
    pl.when(jnp.logical_not(is_low))(above)
    first[0] = first[0] * jnp.where(inside_down, 1.0, 0.0)
    first[tall + 1] = first[tall + 1] * jnp.where(inside_up, 1.0, 0.0)

    for item in token_copies:
        item.wait_send()
    strip_peer.wait_send()
    state_copy.wait_send()

    @pl.when(inner)
    def _():
        strip_mate.wait_send()
        for item in field_copies:
            item.wait_send()

    @pl.when(inside_up)
    def _():
        up_copy.wait_send()

    @pl.when(inside_down)
    def _():
        down_copy.wait_send()


def second_kernel(base, first, out_ref):
    wide = base.shape[2] // 2
    lon = lax.axis_index("lon")
    here = pl.ds(pl.multiple_of(lon * wide, 128), wide)
    there = pl.ds(pl.multiple_of((1 - lon) * wide, 128), wide)
    rows = []
    tall, block = base.shape[0], out_ref.shape[1]
    for k in range(block):
        y = k + pl.program_id(0) * block
        row = base[y]
        if k < 2 or k >= block - 2:
            second = tendency_row(first[y], first[y + 1], first[y + 2])
            done = 0.5 * (row + first[y + 1] + time_step * second)
            row = jnp.where((y < 2) | (y >= tall - 2), done, row)
        rows.append(row)
    value = jnp.swapaxes(jnp.stack(rows), 0, 1)
    out_ref[:, :, here] = value[:, :, 0:wide]
    out_ref[:, :, there] = value[:, :, wide:]


def body(sizes, tokens, ln_gain, w_query, w_keyval, w_out, w_dec, nudge, state):
    cols, width = tokens.shape[1:]
    channels = nudge.shape[0]
    length = state.shape[2] * sizes["lon"]
    tall = state.shape[1] // sizes["lon"]
    windows = cols // WIN
    patches = w_dec.shape[1]
    strip = 16
    chunks = chunk_bounds(windows)
    most = max(w1 - w0 for w0, w1 in chunks)
    count = len(chunks)
    cells = 2 * HALF * WIN
    hbm, vmem = pl.BlockSpec(memory_space=pl.ANY), pl.BlockSpec(memory_space=pltpu.VMEM)
    V = pltpu.VMEM
    edge_rows = V((2, channels, length), BF16)
    pieces = V((count, patches, most * HALF * WIN), BF16)
    scratch = [
        V((width, 3 * width), BF16), V((width, width), BF16), V(w_dec.shape, BF16), V((patches, width), BF16),
        V((length, length), BF16), V((length, length), BF16),
        V((HALF, cols, width), BF16), V((HALF, cols, width), BF16), V((HALF, strip, width), BF16),
        V((HALF * HALF, width), BF16), V((HALF * HALF, width), BF16),
        V((HALF * HALF, width), BF16), V((HALF * HALF, width), BF16),
        V((windows, cells, width), F32), V((windows, HALF * WIN, width), F32),
        V((windows, cells, 3 * width), BF16), V((windows, cells, width), BF16), V((most * cells, width), BF16),
        V((cells, 2 * width // HEADS), F32),
        V((channels, tall, length), F32),
        pieces, pieces, V((HALF * PATCH * channels, length), BF16),
        edge_rows, edge_rows, edge_rows, edge_rows,
        V((channels, 1), F32),
        pltpu.SemaphoreType.DMA((9,)), pltpu.SemaphoreType.DMA((2 * count + 5,)),
        pltpu.SemaphoreType.DMA((2 * count + 5,)),
    ]
    plain, patch, undo = filter_tables(length, KEEP, windows)
    nudged, first = pl.pallas_call(
        functools.partial(cycle_kernel, sizes["lat"], undo),
        out_shape=[
            pltpu.VMEM((tall, channels, length), F32),
            pltpu.VMEM((tall + 2, channels, length), F32),
        ],
        in_specs=[hbm] * 8 + [vmem] * 2,
        out_specs=[vmem, vmem],
        scratch_shapes=scratch,
        compiler_params=pltpu.CompilerParams(
            collective_id=0, has_side_effects=True, vmem_limit_bytes=56 * 2**20
        ),
        name="cycle",
    )(tokens, state, w_query, w_keyval, w_out, w_dec, jnp.asarray(plain), jnp.asarray(patch), ln_gain[None], nudge[None])
    return pl.pallas_call(
        second_kernel,
        out_shape=jax.ShapeDtypeStruct((channels, tall, length), F32),
        grid=(tall // 8,),
        in_specs=[vmem, vmem],
        out_specs=pl.BlockSpec((channels, 8, length), lambda g: (0, g, 0)),
        compiler_params=pltpu.CompilerParams(vmem_limit_bytes=16 * 2**20),
        name="second",
    )(nudged, first)


def solution(mesh):
    in_specs = (
        P(("member", "lat"), "lon", None),
        P(),
        P(),
        P(),
        P(),
        P(),
        P(),
        P(None, ("member", "lat"), "lon"),
    )
    out_specs = P(None, ("member", "lat", "lon"), None)
    return jax.shard_map(
        functools.partial(body, dict(mesh.shape)),
        mesh=mesh,
        in_specs=in_specs,
        out_specs=out_specs,
        check_vma=False,
    )
```
